32 devices in a mesh: grp: 1, date: 4 (over y, x), shard: 8 (over z, core).
Axes of the slice: x: 2, y: 2, z: 4, core: 2. Of those that a mesh axis runs over, the one named last changes fastest.
Arguments:
- echo_spectra: bfloat16 [4, 2, 128, 8192], P(('grp', 'date'), None, 'shard'), may hold values from -6 to 6
- range_reference: float32 [2, 8192], replicated, may hold values from -5 to 5
- azimuth_reference: bfloat16 [2, 128, 8192], P(None, None, 'shard'), may hold values from -5 to 5
- block_owner: int32 [4, 64], P(('grp', 'date')), may hold values from 0 to 7, as said below
- block_slot: int32 [4, 64], P(('grp', 'date')), may hold values from 0 to 15, as said below
- kernel_index: int32 [4, 64], P(('grp', 'date')), may hold values from 0 to 7
Outputs:
- filtered: bfloat16 [4, 128, 2, 2, 128, 128], P(('grp', 'date'), 'shard')
The draws below stay inside these ranges and needn't reach their ends.
Inputs may be any that keep to these rules, and one draw needn't show every extreme that they name: `block_owner`: every date carries the same owners (the stack is coregistered onto one map grid). Within a date, the 8 blocks of one range-column group name any one owner at most 2 times, and some group names some owner exactly 2 times; every owner is named by at most 16 blocks, and some owner by exactly 16. `block_slot`: every date carries the same slots. Within a date, blocks that name the same owner have distinct slots.
All inputs are finite; a program needn't handle non-finite values.
Results may differ from the reference program's by a relative error of at most 0.017.
Values may be sent and summed in bfloat16 or wider, within the bound.
A program may use at most 128 MiB of HBM per device.

```python
import math
import jax
import jax.numpy as jnp
from jax import lax

RNG = 8192
RSPLIT = 64
BLK = 128
NSUB = 8
DATES = 4
PULSES = 128
BLK_DEV = 8
BLOCKS = 64
MOST = 2
CAP = 16
TILES = 128
N_SHARD = 8


def slot_shuffle(perm_key):
    return jax.random.permutation(perm_key, CAP).astype(jnp.int32)


def local_shuffle(perm_key):
    return jax.random.permutation(perm_key, BLK_DEV).astype(jnp.int32)


def plan_grid(grid_key):
    keys = jax.random.split(grid_key, 4)
    extra = CAP - BLK_DEV
    swing = jax.random.randint(keys[0], (N_SHARD // 2,), 0, extra + 1).astype(jnp.int32)
    swing = swing.at[0].set(extra)
    loads = jnp.stack([BLK_DEV + swing, BLK_DEV - swing], axis=1).reshape(N_SHARD)
    order = jax.random.permutation(keys[1], N_SHARD).astype(jnp.int32)
    ends = jnp.cumsum(loads).astype(jnp.int32)
    starts = ends - loads
    place = jnp.arange(BLOCKS, dtype=jnp.int32)
    segment = jnp.sum((place[:, None] >= ends[None, :]).astype(jnp.int32), axis=1)
    owner = order[segment]
    rank = place - starts[segment]
    sender = place // MOST % N_SHARD
    local = place // (MOST * N_SHARD) * MOST + place % MOST
    slot_perms = jax.vmap(slot_shuffle)(jax.random.split(keys[2], N_SHARD))
    slot = slot_perms[owner, rank]
    local_perms = jax.vmap(local_shuffle)(jax.random.split(keys[3], N_SHARD))
    target = sender * BLK_DEV + local_perms[sender, local]
    owners = jnp.zeros((BLOCKS,), jnp.int32).at[target].set(owner)
    slots = jnp.zeros((BLOCKS,), jnp.int32).at[target].set(slot)
    return (owners, slots)


def block_plan(key):
    base = jax.random.fold_in(key, 11)
    owners, slots = plan_grid(base)
    return (jnp.broadcast_to(owners[None, :], (DATES, BLOCKS)), jnp.broadcast_to(slots[None, :], (DATES, BLOCKS)))


def draw_block_owner(key, part):
    return block_plan(key)[0]


def draw_block_slot(key, part):
    return block_plan(key)[1]


def with_ends(array, rng, least, high):
    index_at = [jax.random.randint(jax.random.fold_in(rng, axis), (), 0, length) for axis, length in enumerate(array.shape)]
    widest = array.shape.index(max(array.shape))
    neighbour = index_at[:widest] + [(index_at[widest] + 1) % array.shape[widest]] + index_at[widest + 1:]
    return array.at[tuple(index_at)].set(least).at[tuple(neighbour)].set(high)


def shard_levels(key, dims, pieces, smallest, top_value):
    level = 1.0
    for axis_at, blocks in pieces:
        draws = jax.random.uniform(jax.random.fold_in(jax.random.fold_in(key, 6), axis_at), (blocks,), jnp.float32, smallest / len(pieces), top_value / len(pieces))
        level = level * jnp.repeat(jnp.exp(draws), dims[axis_at] // blocks).reshape((-1,) + (1,) * (len(dims) - 1 - axis_at))
    return level


def gaussian(key, dims, deviation, limit, pieces=(), held_as=jnp.bfloat16):
    result = deviation * jax.random.normal(key, dims, jnp.float32)
    if pieces:
        result = result * shard_levels(key, dims, pieces, -0.22, 0.18)
    return jnp.clip(result, -limit, limit).astype(held_as)


def setup_inputs(seed: int = 0, part: int = 0) -> dict:
    key_of = jax.random.split(jax.random.key(seed), 7)
    part_keys = jax.random.split(jax.random.fold_in(key_of[6], part), 7)
    echo_spectra = gaussian(part_keys[0], (DATES, 2, PULSES, RNG), 1.0, 6.0, ((0, 4), (2, 8)))
    range_reference = gaussian(key_of[1], (2, RNG), 0.7, 5.0, (), jnp.float32)
    azimuth_reference = gaussian(key_of[2], (2, PULSES, RNG), 0.7, 5.0, ((2, 8),))
    block_owner = draw_block_owner(jax.random.fold_in(jax.random.fold_in(key_of[6], part), 71), part)
    block_slot = draw_block_slot(jax.random.fold_in(jax.random.fold_in(key_of[6], part), 71), part)
    kernel_index = with_ends(jax.random.randint(part_keys[5], (DATES, BLOCKS), 0, NSUB), jax.random.fold_in(part_keys[5], 1), 0, NSUB - 1).astype(jnp.int32)
    return {"echo_spectra": echo_spectra, "range_reference": range_reference, "azimuth_reference": azimuth_reference, "block_owner": block_owner, "block_slot": block_slot, "kernel_index": kernel_index}


def dft_block(size, sign):
    index = jnp.arange(size, dtype=jnp.int32)
    phase = index[:, None] * index[None, :] % size
    angle = 2.0 * math.pi / size * phase.astype(jnp.float32)
    scale = 1.0 / math.sqrt(size)
    cosine = jnp.cos(angle) * scale
    sine = sign * jnp.sin(angle) * scale
    table = jnp.stack([jnp.stack([cosine, -sine]), jnp.stack([sine, cosine])])
    return jnp.transpose(table, (0, 2, 1, 3)).astype(jnp.bfloat16)

def twiddle(first_len, second_len, total):
    left = jnp.arange(first_len, dtype=jnp.int32)
    right = jnp.arange(second_len, dtype=jnp.int32)
    phase = left[:, None] * right[None, :] % total
    angle = 2.0 * math.pi / total * phase.astype(jnp.float32)
    return (jnp.cos(angle), jnp.sin(angle))

def kernel_table():
    offset = (jnp.arange(NSUB, dtype=jnp.float32) + 0.5) / NSUB
    cells = jnp.arange(BLK, dtype=jnp.float32)
    dist = cells[None, None, :] - cells[None, :, None] - offset[:, None, None]
    window = jnp.where(jnp.abs(dist) < 4.0, 0.5 + 0.5 * jnp.cos(math.pi * dist / 4.0), 0.0)
    return (jnp.sinc(dist) * window).astype(jnp.bfloat16)

def fdot(form, left, right):
    return jnp.einsum(form, left.astype(jnp.float32), right.astype(jnp.float32))

def range_compress(spectra, reference):
    real_in = spectra[0].astype(jnp.float32)
    imag_in = spectra[1].astype(jnp.float32)
    matched = jnp.stack([real_in * reference[0] + imag_in * reference[1], imag_in * reference[0] - real_in * reference[1]]).astype(jnp.bfloat16)
    count = spectra.shape[1]
    outer_len = RSPLIT
    inner_len = RNG // RSPLIT
    shaped = matched.reshape(2, count, outer_len, inner_len)
    section = fdot('cnek,epkb->cpnb', dft_block(outer_len, 1), shaped)
    twc, tws = twiddle(outer_len, inner_len, RNG)
    first = jnp.stack([section[0] * twc - section[1] * tws, section[0] * tws + section[1] * twc]).astype(jnp.bfloat16)
    second = fdot('cmek,epnk->cpmn', dft_block(inner_len, 1), first)
    return second.reshape(2, count, RNG).astype(jnp.bfloat16)

def azimuth_focus(columns, reference):
    count = columns.shape[1]
    doppler = fdot('cuep,epk->cuk', dft_block(count, -1), columns)
    ref_re = reference[0].astype(jnp.float32)
    ref_im = reference[1].astype(jnp.float32)
    shaped = jnp.stack([doppler[0] * ref_re - doppler[1] * ref_im, doppler[0] * ref_im + doppler[1] * ref_re]).astype(jnp.bfloat16)
    return fdot('cuep,epk->cuk', dft_block(count, 1), shaped).astype(jnp.bfloat16)

def cross(first, second):
    fre = first[:, 0].astype(jnp.float32)
    fim = first[:, 1].astype(jnp.float32)
    sre = second[:, 0].astype(jnp.float32)
    sim = second[:, 1].astype(jnp.float32)
    return jnp.stack([fre * sre + fim * sim, fim * sre - fre * sim], axis=1)

def goldstein(patches):
    forward = dft_block(BLK, -1)
    backward = dft_block(BLK, 1)
    rows = fdot('cuei,npeij->npcuj', forward, patches).astype(jnp.bfloat16)
    spectrum = fdot('npeuj,cvej->npcuv', rows, forward)
    power = spectrum[:, :, 0] ** 2 + spectrum[:, :, 1] ** 2
    smooth = jnp.zeros_like(power)
    for down in (-1, 0, 1):
        for across in (-1, 0, 1):
            smooth = smooth + jnp.roll(power, (down, across), axis=(-2, -1))
    smooth = smooth / 9.0
    level = lax.optimization_barrier(jnp.mean(smooth, axis=(-2, -1), keepdims=True))
    weight = jnp.sqrt(jnp.sqrt(smooth / (level + 1e-06)))
    weighted = (spectrum * weight[:, :, None]).astype(jnp.bfloat16)
    back = fdot('cuei,npeij->npcuj', backward, weighted).astype(jnp.bfloat16)
    return fdot('npeuj,cvej->npcuv', back, backward).astype(jnp.bfloat16)

def date_tiles(spectra, range_reference, azimuth_reference, owners, slots, kinds):
    compressed = range_compress(spectra, range_reference)
    image = azimuth_focus(compressed, azimuth_reference)
    row_blocks = PULSES // BLK
    col_blocks = RNG // (N_SHARD * BLK)
    blocks = image.reshape(2, row_blocks, BLK, N_SHARD, col_blocks, BLK)
    blocks = jnp.transpose(blocks, (3, 1, 4, 0, 2, 5)).reshape(BLOCKS, 2, BLK, BLK)
    kernels = kernel_table()[kinds]
    resampled = fdot('nij,ncjk->ncik', kernels, blocks).astype(jnp.bfloat16)
    tiles = jnp.zeros((TILES, 2, BLK, BLK), jnp.bfloat16)
    return tiles.at[owners * CAP + slots].set(resampled)

def reference(echo_spectra, range_reference, azimuth_reference, block_owner, block_slot, kernel_index):
    mapped = [date_tiles(echo_spectra[d], range_reference, azimuth_reference, block_owner[d], block_slot[d], kernel_index[d]) for d in range(DATES)]
    results = []
    for d in range(DATES):
        pairs = jnp.stack([cross(mapped[d], mapped[(d + 1) % DATES]), cross(mapped[d], mapped[(d + 2) % DATES])], axis=1).astype(jnp.bfloat16)
        grouped = pairs.reshape(N_SHARD, CAP, 2, 2, BLK, BLK)
        done = lax.map(goldstein, grouped)
        results.append(done.reshape(TILES, 2, 2, BLK, BLK))
    return jnp.stack(results)
```

```python
import functools
import math

import jax
import jax.numpy as jnp
import ml_dtypes
import numpy as np
from jax import lax
from jax.experimental import pallas as pl
from jax.experimental.pallas import tpu as pltpu
from jax.sharding import PartitionSpec as P

BLK = 128
NSUB = 8
BF = jnp.bfloat16
F32 = jnp.float32


def dft_parts(size, sign):
    index = np.arange(size)
    angle = 2.0 * math.pi / size * (index[:, None] * index[None, :] % size)
    scale = 1.0 / math.sqrt(size)
    return np.cos(angle) * scale, sign * np.sin(angle) * scale


def left_table(size, sign):
    cosine, sine = dft_parts(size, sign)
    return np.block([[cosine, -sine], [sine, cosine]]).astype(ml_dtypes.bfloat16)


def right_table(size, sign):
    return np.ascontiguousarray(left_table(size, sign).T)


def first_table(rng):
    outer, inner = BLK, rng // BLK
    low = outer * BLK // rng
    cosine, sine = dft_parts(outer, 1)
    full = np.stack([np.stack([cosine, sine], 1), np.stack([-sine, cosine], 1)])
    full = full.reshape(2, outer // low, low, 2 * outer)
    return np.transpose(full, (2, 0, 1, 3)).reshape(2 * outer, 2 * outer).astype(ml_dtypes.bfloat16)


def twiddle_table(rng):
    inner = rng // BLK
    phase = np.arange(inner)[:, None] * np.arange(BLK)[None, :] % rng
    angle = 2.0 * math.pi / rng * phase
    return np.stack([np.cos(angle), np.sin(angle)]).astype(np.float32)


def kernel_table():
    offset = (np.arange(NSUB) + 0.5) / NSUB
    cells = np.arange(BLK)
    dist = cells[None, None, :] - cells[None, :, None] - offset[:, None, None]
    window = np.where(np.abs(dist) < 4.0, 0.5 + 0.5 * np.cos(math.pi * dist / 4.0), 0.0)
    return (np.sinc(dist) * window).astype(ml_dtypes.bfloat16)


def flipped(a, b, n):
    total = 0
    bit = 1
    while bit < n:
        total = total + (a // bit + b // bit) % 2 * bit
        bit *= 2
    return total


def mm(left, right):
    return jnp.dot(left, right, preferred_element_type=F32)


def kernel(
    n,
    dates,
    most,
    capacity,
    owner_ref,
    slot_ref,
    kinds_ref,
    echo_hbm,
    rref_hbm,
    aref_hbm,
    t1_hbm,
    tw_hbm,
    w2_hbm,
    pf_hbm,
    pb_hbm,
    kt_hbm,
    gfl_hbm,
    gfr_hbm,
    gbl_hbm,
    gbr_hbm,
    fil_hbm,
    entry_ref,
    echo_ref,
    rref_ref,
    t1_ref,
    tw_ref,
    w2_ref,
    pf_ref,
    pb_ref,
    kt_ref,
    gfl_ref,
    gfr_ref,
    gbl_ref,
    gbr_ref,
    ats,
    fil,
    tile_ref,
    kind_ref,
    row_ref,
    lhs,
    mat,
    snd,
    mix,
    xch,
    xin,
    azin,
    azm,
    azf,
    azx0,
    azx1,
    azx2,
    img,
    inbox,
    ybox,
    xbox,
    si,
    sa,
    sw,
    se,
    re,
    sd,
    rd,
    sz,
    rz,
    saz,
    raz,
    sf,
    rf,
    sy,
    ry,
    sx,
    rx,
):
    me = lax.axis_index("shard")
    day = lax.axis_index("date")
    grp = lax.axis_index("grp")
    relay = dates == 4
    parity = lax.rem(day, 2)
    ydst = lax.rem(day + dates - 2, dates)
    xnext = lax.rem(day + dates - 1, dates)
    xdst = day + 1 - 2 * parity if relay else xnext
    mesh_id = pl.DeviceIdType.MESH

    barrier = pltpu.get_barrier_semaphore()

    def greet(k, _):
        pl.semaphore_signal(
            barrier, inc=1, device_id=(grp, day, flipped(me, k, n)), device_id_type=mesh_id
        )
        return 0

    lax.fori_loop(1, n, greet, 0)
    if relay:
        others = [flipped(day, x, dates) for x in range(1, dates)]
    else:
        others = [lax.rem(day + 2, dates), lax.rem(day + 1, dates)]
    for other in others:
        pl.semaphore_signal(barrier, inc=1, device_id=(grp, other, me), device_id_type=mesh_id)

    pulses = echo_ref.shape[1]
    rng = echo_ref.shape[2]
    tiles = rng // BLK
    inner = rng // BLK
    mine = tiles // n
    wide = n * pulses
    rows_of = wide // BLK
    chips = n // 2
    total = n * most
    per = owner_ref.shape[1] // n
    parts = azin.shape[1]
    part = wide // parts
    near = list(range(1, chips // 2 if relay else chips))
    far = list(range(chips // 2, chips)) if relay else []

    loads = [
        pltpu.make_async_copy(a, b, si.at[i])
        for i, (a, b) in enumerate(
            [
                (echo_hbm, echo_ref),
                (rref_hbm, rref_ref),
                (t1_hbm, t1_ref),
                (tw_hbm, tw_ref),
                (w2_hbm, w2_ref),
                (pf_hbm, pf_ref),
                (pb_hbm, pb_ref),
                (kt_hbm, kt_ref),
                (gfl_hbm, gfl_ref),
                (gfr_hbm, gfr_ref),
                (gbl_hbm, gbl_ref),
                (gbr_hbm, gbr_ref),
            ]
        )
    ]
    slabs = [
        pltpu.make_async_copy(aref_hbm.at[:, :, pl.ds(t * BLK, BLK)], ats.at[t], sa.at[t])
        for t in range(mine)
    ]
    for load in loads[:5] + slabs + loads[5:]:
        load.start()

    def sources(i, _):
        dest = flipped(me, i // n, n)
        group = flipped(dest, lax.rem(i, n), n)
        seen = jnp.int32(0)
        found = [jnp.int32(0)] * most
        for b in range(per):
            named = owner_ref[0, group * per + b] == dest
            for r in range(most):
                found[r] = jnp.where(named & (seen == r), b, found[r])
            seen = seen + named.astype(jnp.int32)
        for r in range(most):
            tile_ref[i * most + r] = group * mine + lax.rem(found[r], mine)
            row_ref[i * most + r] = found[r] // mine
            kind_ref[i * most + r] = kinds_ref[0, group * per + found[r]]
        return 0

    lax.fori_loop(0, n * n, sources, 0)

    def entries(t, held):
        held = list(held)
        at = flipped(me, t, n) * most
        for b in range(per):
            named = owner_ref[0, t * per + b] == me
            slot = jnp.where(named, slot_ref[0, t * per + b], -1)
            for q in range(capacity):
                held[q] = jnp.where(slot == q, at, held[q])
            at = at + named.astype(jnp.int32)
        return tuple(held)

    for load in loads[:5]:
        load.wait()
    real = echo_ref[0].astype(F32)
    imag = echo_ref[1].astype(F32)
    rre = rref_ref[0:1, :]
    rim = rref_ref[1:2, :]
    mat[0] = (real * rre + imag * rim).reshape(pulses, tiles, BLK)
    mat[1] = (imag * rre - real * rim).reshape(pulses, tiles, BLK)

    for p in range(pulses):
        both = jnp.concatenate([mat[0, p], mat[1, p]], axis=0).T
        low = BLK // inner
        pieces = [both[x * inner : (x + 1) * inner] for x in range(low)]
        lhs[p * inner : (p + 1) * inner, :] = jnp.concatenate(pieces, axis=1).astype(BF)

    twc = tw_ref[0]
    tws = tw_ref[1]
    group = 4
    for g in range(0, pulses, group):
        section = mm(lhs[g * inner : (g + group) * inner, :], t1_ref[...])
        rights = []
        for p in range(group):
            sre = section[p * inner : (p + 1) * inner, :BLK]
            sim = section[p * inner : (p + 1) * inner, BLK:]
            rights.append(
                jnp.concatenate([sre * twc - sim * tws, sre * tws + sim * twc], axis=0).astype(BF)
            )
        second = mm(w2_ref[...], jnp.concatenate(rights, axis=1))
        for p in range(group):
            mat[:, g + p] = second[:, p * BLK : (p + 1) * BLK].reshape(2, tiles, BLK)
    for c in range(2):
        snd[c] = jnp.swapaxes(mat[c], 0, 1).astype(BF)

    def gather(k, _):
        for zz in range(chips):
            for cc in range(2):
                for r in range(most):
                    piece = snd[:, tile_ref[((2 * zz + cc) * n + k) * most + r]]
                    if cc:
                        xch[zz, k, r] = piece
                    elif zz:
                        mix[0, zz - 1, k, r] = piece
                    else:
                        xin[k, 0, r] = piece
        return 0

    lax.fori_loop(0, n, gather, 0)

    for slab in slabs:
        slab.wait()

    def filters(j, r):
        return ats.at[tile_ref[(j * n + j) * most + r] - me * mine]

    for r in range(most):
        for d in range(parts):
            rows = slice(d * part, (d + 1) * part)
            azin[0, d, r] = filters(0, r)[:, rows]
            azx0[d, r] = filters(1, r)[:, rows]
            for i, zz in enumerate(near):
                azm[0, i, d, r] = filters(2 * zz, r)[:, rows]
                azx1[i, d, r] = filters(2 * zz + 1, r)[:, rows]
        for i, zz in enumerate(far):
            rows = pl.ds(pl.multiple_of(day * part, part), part)
            azf[0, i, r] = filters(2 * zz, r)[:, rows]
            azx2[i, r] = filters(2 * zz + 1, r)[:, rows]

    pl.semaphore_wait(barrier, n - 1 + len(others))

    def remote(src, dst, send, recv, to_day, flip):
        return pltpu.make_async_remote_copy(
            src_ref=src,
            dst_ref=dst,
            send_sem=send,
            recv_sem=recv,
            device_id=(grp, to_day, me if flip is None else flipped(me, flip, n)),
            device_id_type=mesh_id,
        )

    swaps = [
        remote(xch.at[pl.ds(1, chips - 1)], mix.at[1], se.at[0], re.at[0], day, 1),
        remote(xch.at[0], xin.at[:, 1], se.at[1], re.at[1], day, 1),
        remote(azx0, azin.at[1], se.at[2], re.at[2], day, 1),
        remote(azx1, azm.at[1], se.at[3], re.at[3], day, 1),
    ]
    if far:
        swaps.append(remote(azx2, azf.at[1], se.at[4], re.at[4], day, 1))

    def direct(zz, cc):
        i = 2 * (zz - 1) + cc
        src = xch.at[zz, 0] if cc else mix.at[0, zz - 1, 0]
        return remote(src, xin.at[0, 2 * zz + cc], sd.at[i], rd.at[i], day, 2 * zz + cc)

    def step(k, zz):
        return remote(
            mix.at[:, zz - 1, k],
            xin.at[k, pl.ds(2 * zz, 2)],
            sz.at[k, zz - 1],
            rz.at[k, zz - 1],
            day,
            2 * zz,
        )

    def last(r, zz):
        return remote(
            mix.at[:, zz - 1, n - 1, r],
            xin.at[n - 1, pl.ds(2 * zz, 2), r],
            sz.at[n - 1 + r, zz - 1],
            rz.at[n - 1 + r, zz - 1],
            day,
            2 * zz,
        )

    def near_filter(i):
        zz = near[i]
        return remote(
            azm.at[:, i], azin.at[pl.ds(2 * zz, 2)], saz.at[zz - 1], raz.at[zz - 1], day, 2 * zz
        )

    def far_filter(i):
        zz = far[i]
        return remote(
            azf.at[:, i],
            azin.at[pl.ds(2 * zz, 2), day],
            saz.at[zz - 1],
            raz.at[zz - 1],
            day,
            2 * zz,
        )

    def pass_on(x):
        slab = azin.at[pl.ds(n // 2, n // 2), day]
        return remote(slab, slab, sf.at[x - 1], rf.at[x - 1], flipped(day, x, dates), None)

    swaps[0].start()
    swaps[1].start()
    for zz in range(chips - 1, 0, -1):
        for cc in range(2):
            direct(zz, cc).start()
    for swap in swaps[2:]:
        swap.start()
    swaps[0].wait_recv()
    for zz in range(chips - 1, 0, -1):
        step(1, zz).start()
    for swap in swaps[3:]:
        swap.wait_recv()
    for i in range(len(far)):
        far_filter(i).start()
    for i in range(len(near)):
        near_filter(i).start()

    def start_step(k, _):
        for zz in range(chips - 1, 0, -1):
            step(k, zz).start()
        return 0

    lax.fori_loop(2, n - 1, start_step, 0)
    for r in range(most):
        for zz in range(chips - 1, 0, -1):
            last(r, zz).start()

    held = lax.fori_loop(0, n, entries, (jnp.int32(total),) * capacity)
    for q in range(capacity):
        entry_ref[q] = held[q]
    fil[total] = jnp.zeros_like(fil[total])

    def write(e):
        return pltpu.make_async_copy(fil.at[e], fil_hbm.at[e], sw.at[e])

    write(total).start()
    for load in loads[5:]:
        load.wait()

    def copy_y(e):
        return remote(inbox.at[e], ybox.at[e], sy.at[e], ry.at[e], ydst, None)

    def copy_x(e, source, to):
        return remote(source.at[e], xbox.at[e], sx.at[e], rx.at[e], to, None)

    def focus(k, picks):
        columns = []
        filt = []
        for r in picks:
            pieces = [
                xin[k, flipped(me, s, n), r, c] for c in range(2) for s in range(n)
            ]
            columns.append(jnp.concatenate(pieces, axis=0))
            filt.append(
                [
                    jnp.concatenate([azin[k, d, r, c] for d in range(parts)], axis=0)
                    for c in range(2)
                ]
            )
        doppler = mm(pf_ref[...], jnp.concatenate(columns, axis=1))
        are = jnp.concatenate([f[0] for f in filt], axis=1).astype(F32)
        aim = jnp.concatenate([f[1] for f in filt], axis=1).astype(F32)
        dre = doppler[:wide]
        dim = doppler[wide:]
        shaped = jnp.concatenate([dre * are - dim * aim, dre * aim + dim * are], axis=0).astype(BF)
        image = mm(pb_ref[...], shaped).astype(BF)
        for i, r in enumerate(picks):
            e = k * most + r
            block = [
                jnp.concatenate(
                    [
                        image[c * wide + y * BLK : c * wide + (y + 1) * BLK, i * BLK : (i + 1) * BLK]
                        for c in range(2)
                    ],
                    axis=1,
                )
                for y in range(rows_of)
            ]
            if rows_of > 1:
                for y in range(rows_of):
                    img[i, y] = block[y]
                block = [img[i, row_ref[e]]]
            inbox[e] = mm(kt_ref[kind_ref[e]], block[0]).astype(BF)

    def stage_a(k):
        @pl.when(k == 0)
        def _():
            swaps[1].wait_recv()
            for zz in range(1, chips):
                for cc in range(2):
                    direct(zz, cc).wait_recv()

        @pl.when(k > 0)
        def _():
            for zz in range(1, chips):
                step(k, zz).wait_recv()

        @pl.when(k == 1)
        def _():
            swaps[2].wait_recv()

        for i, zz in enumerate(near):

            @pl.when(k == 2 * zz)
            def _():
                near_filter(i).wait_recv()

        if far:

            @pl.when(k == n // 2)
            def _():
                for x in range(1, dates):
                    pass_on(x).wait_recv()

        focus(k, range(most))
        for r in range(most):
            e = k * most + r
            copy_y(e).start()
            if relay:

                @pl.when(parity == 1)
                def _():
                    copy_x(e, inbox, xdst).start()
            else:
                copy_x(e, inbox, xdst).start()

    def stage_b(e):
        copy_y(e).wait_recv()
        if relay:

            @pl.when(parity == 0)
            def _():
                copy_x(e, ybox, xdst).start()

    def patches(at):
        own = inbox[at].astype(F32)
        ore = own[:, :BLK]
        oim = own[:, BLK:]
        tops = []
        lows = []
        for box in (xbox, ybox):
            oth = box[at].astype(F32)
            tre = oth[:, :BLK]
            tim = oth[:, BLK:]
            tops.append(ore * tre + oim * tim)
            lows.append(oim * tre - ore * tim)
        pair = jnp.concatenate(
            [jnp.concatenate(tops, axis=1), jnp.concatenate(lows, axis=1)], axis=0
        ).astype(BF)

        def turned(x):
            return jnp.concatenate(
                [
                    jnp.concatenate([x[:BLK, :BLK], x[BLK:, :BLK]], axis=1),
                    jnp.concatenate([x[:BLK, BLK:], x[BLK:, BLK:]], axis=1),
                ],
                axis=0,
            )

        rows = mm(gfl_ref[...], pair).astype(BF)
        spectrum = mm(turned(rows), gfr_ref[...])
        weighted = []
        for x in range(2):
            spec = spectrum[x * BLK : (x + 1) * BLK]
            sre = spec[:, :BLK]
            sim = spec[:, BLK:]
            power = sre * sre + sim * sim
            line = power + pltpu.roll(power, 1, 1) + pltpu.roll(power, BLK - 1, 1)
            smooth = (line + pltpu.roll(line, 1, 0) + pltpu.roll(line, BLK - 1, 0)) * (1.0 / 9.0)
            level = jnp.sum(jnp.sum(smooth, axis=0, keepdims=True), axis=1, keepdims=True)
            level = level * (1.0 / (BLK * BLK)) + 1e-06
            weight = lax.rsqrt(lax.rsqrt(smooth * (1.0 / level)))
            weighted.append(jnp.concatenate([sre * weight, sim * weight], axis=1))
        weighted = jnp.concatenate(weighted, axis=0).astype(BF)
        back = mm(gbl_ref[...], turned(weighted)).astype(BF)
        done = mm(turned(back), gbr_ref[...]).astype(BF)
        for x in range(2):
            for c in range(2):
                fil[at, x, c] = done[x * BLK : (x + 1) * BLK, c * BLK : (c + 1) * BLK]

    def stage_c(e):
        copy_x(e, inbox, xdst).wait_recv()
        patches(e)
        write(e).start()

    def many(stage, first, stop):
        def one(e, _):
            stage(e)
            return 0

        lax.fori_loop(first, stop, one, 0)

    def main(t, _):
        stage_a(t)

        @pl.when(t > 2)
        def _():
            stage_c((t - 3) * most)

        @pl.when(t > 0)
        def _():
            for r in range(most):
                stage_b((t - 1) * most + r)

        if far:

            @pl.when(t == 1)
            def _():
                for i in range(len(far)):
                    far_filter(i).wait_recv()
                for x in range(1, dates):
                    pass_on(x).start()

        @pl.when(t > 2)
        def _():
            many(stage_c, (t - 3) * most + 1, (t - 2) * most)

        return 0

    lax.fori_loop(0, n - 1, main, 0)
    for r in range(most):
        for zz in range(1, chips):
            last(r, zz).wait_recv()
        focus(n - 1, [r])
        e = (n - 1) * most + r
        copy_y(e).start()
        copy_x(e, inbox, xnext).start()

    def closing(r, _):
        stage_c((n - 4) * most + r)
        stage_b((n - 2) * most + r)
        return 0

    lax.fori_loop(0, most, closing, 0)
    many(stage_c, (n - 3) * most, (n - 1) * most)

    def final(e):
        copy_y(e).wait_recv()
        stage_c(e)

    many(final, (n - 1) * most, total)

    def drain(k, _):
        copy_y(k).wait_send()
        copy_x(k, inbox, xdst).wait_send()
        return 0

    for swap in swaps:
        swap.wait_send()
    for zz in range(1, chips):
        for cc in range(2):
            direct(zz, cc).wait_send()
        for r in range(most):
            last(r, zz).wait_send()

    def drain_step(k, _):
        for zz in range(1, chips):
            step(k, zz).wait_send()
        return 0

    lax.fori_loop(1, n - 1, drain_step, 0)
    for i in range(len(near)):
        near_filter(i).wait_send()
    for i in range(len(far)):
        far_filter(i).wait_send()
    if far:
        for x in range(1, dates):
            pass_on(x).wait_send()
    lax.fori_loop(0, total, drain, 0)

    def written(k, _):
        write(k).wait()
        return 0

    lax.fori_loop(0, total + 1, written, 0)


def place(capacity, entry_ref, fil_hbm, out_ref, fil, reads, sems):
    def read(q):
        return pltpu.make_async_copy(fil_hbm.at[entry_ref[q]], fil.at[q], reads.at[q])

    def copy(q):
        return pltpu.make_async_copy(fil.at[q], out_ref.at[q], sems.at[q])

    for q in range(capacity):
        read(q).start()
    for q in range(capacity):
        read(q).wait()
        copy(q).start()
    for q in range(capacity):
        copy(q).wait()


def body(dates, echo_spectra, range_reference, azimuth_reference, block_owner, block_slot, kernel_index):
    n = lax.axis_size("shard")
    per = block_owner.shape[1] // n
    most = max(2, 2 * per // n)
    capacity = min(2 * per, n * most)
    echo = echo_spectra[0]
    pulses, rng = echo.shape[1:]
    inner = rng // BLK
    mine = rng // BLK // n
    wide = pulses * n
    chips = n // 2
    relay = dates == 4
    parts = dates if relay else 1
    part = wide // parts
    near = (chips // 2 if relay else chips) - 1
    far = chips - 1 - near
    tables = [
        first_table(rng),
        twiddle_table(rng),
        left_table(inner, 1),
        left_table(wide, -1),
        left_table(wide, 1),
        kernel_table(),
        left_table(BLK, -1),
        right_table(BLK, -1),
        left_table(BLK, 1),
        right_table(BLK, 1),
    ]
    smem = pl.BlockSpec(memory_space=pltpu.SMEM)
    hbm = pl.BlockSpec(memory_space=pl.ANY)
    total = n * most
    box = pltpu.VMEM((total, BLK, 2 * BLK), BF)
    dma = pltpu.SemaphoreType.DMA
    tables = [jnp.asarray(t) for t in tables]
    operands = [block_owner, block_slot, kernel_index, echo, range_reference, azimuth_reference]
    operands += tables
    held = [echo, range_reference] + tables
    filtered, entry = pl.pallas_call(
        functools.partial(kernel, n, dates, most, capacity),
        out_shape=(
            jax.ShapeDtypeStruct((total + 1, 2, 2, BLK, BLK), BF),
            jax.ShapeDtypeStruct((capacity,), jnp.int32),
        ),
        in_specs=[smem] * 3 + [hbm] * 13,
        out_specs=(hbm, smem),
        scratch_shapes=[pltpu.VMEM(a.shape, a.dtype) for a in held]
        + [
            pltpu.VMEM((mine, 2, wide, BLK), BF),
            pltpu.VMEM((total + 1, 2, 2, BLK, BLK), BF),
            pltpu.SMEM((n * total,), jnp.int32),
            pltpu.SMEM((n * total,), jnp.int32),
            pltpu.SMEM((n * total,), jnp.int32),
            pltpu.VMEM((pulses * inner, 2 * BLK), BF),
            pltpu.VMEM((2, pulses, rng // BLK, BLK), F32),
            pltpu.VMEM((2, rng // BLK, pulses, BLK), BF),
            pltpu.VMEM((2, chips - 1, n, most, 2, pulses, BLK), BF),
            pltpu.VMEM((chips, n, most, 2, pulses, BLK), BF),
            pltpu.VMEM((n, n, most, 2, pulses, BLK), BF),
            pltpu.VMEM((n, parts, most, 2, part, BLK), BF),
            pltpu.VMEM((2, near, parts, most, 2, part, BLK), BF),
            pltpu.VMEM((2, max(far, 1), most, 2, part, BLK), BF),
            pltpu.VMEM((parts, most, 2, part, BLK), BF),
            pltpu.VMEM((near, parts, most, 2, part, BLK), BF),
            pltpu.VMEM((max(far, 1), most, 2, part, BLK), BF),
            pltpu.VMEM((most, wide // BLK, BLK, 2 * BLK), BF),
            box,
            box,
            box,
            dma((len(held),)),
            dma((mine,)),
            dma((total + 1,)),
            *[dma((5,))] * 2,
            *[dma((2 * (chips - 1),))] * 2,
            *[dma((n - 1 + most, chips - 1))] * 2,
            *[dma((chips - 1,))] * 2,
            *[dma((dates - 1,))] * 2,
            *[dma((total,))] * 4,
        ],
        compiler_params=pltpu.CompilerParams(collective_id=0, has_side_effects=True),
    )(
        *operands
    )
    out = pl.pallas_call(
        functools.partial(place, capacity),
        out_shape=jax.ShapeDtypeStruct((capacity, 2, 2, BLK, BLK), BF),
        in_specs=[smem, hbm],
        out_specs=hbm,
        scratch_shapes=[
            pltpu.VMEM((capacity, 2, 2, BLK, BLK), BF),
            dma((capacity,)),
            dma((capacity,)),
        ],
    )(entry, filtered)
    return out[None]


def solution(mesh):
    in_specs = (
        P(("grp", "date"), None, "shard", None),
        P(),
        P(None, None, "shard"),
        P(("grp", "date"), None),
        P(("grp", "date"), None),
        P(("grp", "date"), None),
    )
    out_specs = P(("grp", "date"), "shard", None, None, None, None)
    return jax.shard_map(
        functools.partial(body, mesh.shape["date"]),
        mesh=mesh,
        in_specs=in_specs,
        out_specs=out_specs,
        check_vma=False,
    )
```

```python
import functools
import math

import jax
import jax.numpy as jnp
import ml_dtypes
import numpy as np
from jax import lax
from jax.experimental import pallas as pl
from jax.experimental.pallas import tpu as pltpu
from jax.sharding import PartitionSpec as P

BLK = 128
NSUB = 8
WORD = 4
BF = jnp.bfloat16
F32 = jnp.float32


def dft_parts(size, sign):
    index = np.arange(size)
    angle = 2.0 * math.pi / size * (index[:, None] * index[None, :] % size)
    scale = 1.0 / math.sqrt(size)
    return np.cos(angle) * scale, sign * np.sin(angle) * scale


def left_table(size, sign):
    cosine, sine = dft_parts(size, sign)
    return np.block([[cosine, -sine], [sine, cosine]]).astype(ml_dtypes.bfloat16)


def right_table(size, sign):
    return np.ascontiguousarray(left_table(size, sign).T)


def first_table(rng):
    outer, inner = BLK, rng // BLK
    low = outer * BLK // rng
    cosine, sine = dft_parts(outer, 1)
    full = np.stack([np.stack([cosine, sine], 1), np.stack([-sine, cosine], 1)])
    full = full.reshape(2, outer // low, low, 2 * outer)
    return np.transpose(full, (2, 0, 1, 3)).reshape(2 * outer, 2 * outer).astype(ml_dtypes.bfloat16)


def twiddle_table(rng):
    inner = rng // BLK
    phase = np.arange(inner)[:, None] * np.arange(BLK)[None, :] % rng
    angle = 2.0 * math.pi / rng * phase
    return np.stack([np.cos(angle), np.sin(angle)]).astype(np.float32)


def kernel_table():
    offset = (np.arange(NSUB) + 0.5) / NSUB
    cells = np.arange(BLK)
    dist = cells[None, None, :] - cells[None, :, None] - offset[:, None, None]
    window = np.where(np.abs(dist) < 4.0, 0.5 + 0.5 * np.cos(math.pi * dist / 4.0), 0.0)
    return (np.sinc(dist) * window).astype(ml_dtypes.bfloat16)


def flipped(a, b, n):
    total = 0
    bit = 1
    while bit < n:
        total = total + (a // bit + b // bit) % 2 * bit
        bit *= 2
    return total


def mm(left, right):
    return jnp.dot(left, right, preferred_element_type=F32)


def kernel(
    n,
    dates,
    most,
    capacity,
    owner_ref,
    slot_ref,
    kinds_ref,
    echo_hbm,
    rref_hbm,
    aref_hbm,
    t1_hbm,
    tw_hbm,
    w2_hbm,
    pf_hbm,
    pb_hbm,
    kt_hbm,
    gfl_hbm,
    gfr_hbm,
    gbl_hbm,
    gbr_hbm,
    fil,
    entry_ref,
    echo_ref,
    rref_ref,
    t1_ref,
    tw_ref,
    w2_ref,
    pf_ref,
    pb_ref,
    kt_ref,
    gfl_ref,
    gfr_ref,
    gbl_ref,
    gbr_ref,
    ats,
    tile_ref,
    kind_ref,
    row_ref,
    lhs,
    mat,
    snd,
    mix,
    xch,
    xin,
    azin,
    azm,
    azf,
    azx0,
    azx1,
    azx2,
    img,
    inbox,
    ybox,
    xbox,
    si,
    sa,
    se,
    re,
    sd,
    rd,
    sz,
    rz,
    saz,
    raz,
    sf,
    rf,
    sy,
    ry,
    sx,
    rx,
):
    me = lax.axis_index("shard")
    day = lax.axis_index("date")
    grp = lax.axis_index("grp")
    relay = dates == 4
    parity = lax.rem(day, 2)
    ydst = lax.rem(day + dates - 2, dates)
    xnext = lax.rem(day + dates - 1, dates)
    xdst = day + 1 - 2 * parity if relay else xnext
    mesh_id = pl.DeviceIdType.MESH

    barrier = pltpu.get_barrier_semaphore()

    def greet(k, _):
        pl.semaphore_signal(
            barrier, inc=1, device_id=(grp, day, flipped(me, k, n)), device_id_type=mesh_id
        )
        return 0

    lax.fori_loop(1, n, greet, 0)
    if relay:
        others = [flipped(day, x, dates) for x in range(1, dates)]
    else:
        others = [lax.rem(day + 2, dates), lax.rem(day + 1, dates)]
    for other in others:
        pl.semaphore_signal(barrier, inc=1, device_id=(grp, other, me), device_id_type=mesh_id)

    pulses = echo_ref.shape[1]
    rng = echo_ref.shape[2]
    tiles = rng // BLK
    inner = rng // BLK
    mine = tiles // n
    wide = n * pulses
    rows_of = wide // BLK
    chips = n // 2
    total = n * most
    per = owner_ref.shape[1] // n
    parts = azin.shape[1]
    part = wide // parts
    near = list(range(1, chips // 2 if relay else chips))
    far = list(range(chips // 2, chips)) if relay else []

    loads = [
        pltpu.make_async_copy(a, b, si.at[i])
        for i, (a, b) in enumerate(
            [
                (echo_hbm, echo_ref),
                (rref_hbm, rref_ref),
                (t1_hbm, t1_ref),
                (tw_hbm, tw_ref),
                (w2_hbm, w2_ref),
                (pf_hbm, pf_ref),
                (pb_hbm, pb_ref),
                (kt_hbm, kt_ref),
                (gfl_hbm, gfl_ref),
                (gfr_hbm, gfr_ref),
                (gbl_hbm, gbl_ref),
                (gbr_hbm, gbr_ref),
            ]
        )
    ]
    slabs = [
        pltpu.make_async_copy(aref_hbm.at[:, :, pl.ds(t * BLK, BLK)], ats.at[t], sa.at[t])
        for t in range(mine)
    ]
    for load in loads[:5] + slabs + loads[5:]:
        load.start()

    bits = 32 // WORD
    words = (n + bits - 1) // bits

    def sources(g, _):
        packed = [[jnp.int32(0)] * most for _ in range(words)]
        for b in range(per):
            owner = owner_ref[0, g * per + b]
            for w in range(words):
                shift = (owner - w * bits) * WORD
                live = None
                if words > 1:
                    live = owner // bits == w
                    shift = jnp.where(live, shift, 0)
                for r in range(most):
                    empty = ((packed[w][r] >> shift) & (2**WORD - 1)) == 0
                    put = empty if live is None else live & empty
                    packed[w][r] = packed[w][r] | jnp.where(put, (b + 1) << shift, 0)
                    live = ~empty if live is None else live & ~empty
        for w in range(words):
            for x in range(w * bits, min(n, (w + 1) * bits)):
                flip = flipped(me, x, n)
                for r in range(most):
                    found = (packed[w][r] >> ((x - w * bits) * WORD)) & (2**WORD - 1)
                    found = jnp.maximum(found - 1, 0)
                    tile_ref[(flip * n + flipped(g, x, n)) * most + r] = g * mine + lax.rem(found, mine)
        return 0

    lax.fori_loop(0, n, sources, 0)

    def entries(t, held):
        held = list(held)
        at = flipped(me, t, n) * most
        found = [jnp.int32(0)] * most
        seen = jnp.int32(0)
        for b in range(per):
            named = owner_ref[0, t * per + b] == me
            for r in range(most):
                found[r] = jnp.where(named & (seen == r), b, found[r])
            seen = seen + named.astype(jnp.int32)
        for r in range(most):
            row_ref[at + r] = found[r] // mine
            kind_ref[at + r] = kinds_ref[0, t * per + found[r]]
        for b in range(per):
            named = owner_ref[0, t * per + b] == me
            slot = jnp.where(named, slot_ref[0, t * per + b], -1)
            for q in range(capacity):
                held[q] = jnp.where(slot == q, at, held[q])
            at = at + named.astype(jnp.int32)
        return tuple(held)

    for load in loads[:5]:
        load.wait()
    real = echo_ref[0].astype(F32)
    imag = echo_ref[1].astype(F32)
    rre = rref_ref[0:1, :]
    rim = rref_ref[1:2, :]
    mat[0] = (real * rre + imag * rim).reshape(pulses, tiles, BLK)
    mat[1] = (imag * rre - real * rim).reshape(pulses, tiles, BLK)

    for p in range(pulses):
        both = jnp.concatenate([mat[0, p], mat[1, p]], axis=0).T
        low = BLK // inner
        pieces = [both[x * inner : (x + 1) * inner] for x in range(low)]
        lhs[p * inner : (p + 1) * inner, :] = jnp.concatenate(pieces, axis=1).astype(BF)

    twc = tw_ref[0]
    tws = tw_ref[1]
    group = 4
    for g in range(0, pulses, group):
        section = mm(lhs[g * inner : (g + group) * inner, :], t1_ref[...])
        rights = []
        for p in range(group):
            sre = section[p * inner : (p + 1) * inner, :BLK]
            sim = section[p * inner : (p + 1) * inner, BLK:]
            rights.append(
                jnp.concatenate([sre * twc - sim * tws, sre * tws + sim * twc], axis=0).astype(BF)
            )
        second = mm(w2_ref[...], jnp.concatenate(rights, axis=1))
        for p in range(group):
            mat[:, g + p] = second[:, p * BLK : (p + 1) * BLK].reshape(2, tiles, BLK)
    for c in range(2):
        snd[c] = jnp.swapaxes(mat[c], 0, 1).astype(BF)

    def gather(k, _):
        for zz in range(chips):
            for cc in range(2):
                for r in range(most):
                    piece = snd[:, tile_ref[((2 * zz + cc) * n + k) * most + r]]
                    if cc:
                        xch[zz, k, r] = piece
                    elif zz:
                        mix[0, zz - 1, k, r] = piece
                    else:
                        xin[k, 0, r] = piece
        return 0

    lax.fori_loop(0, n, gather, 0)

    for slab in slabs:
        slab.wait()

    def filters(j, r):
        return ats.at[tile_ref[(j * n + j) * most + r] - me * mine]

    for r in range(most):
        for d in range(parts):
            rows = slice(d * part, (d + 1) * part)
            azin[0, d, r] = filters(0, r)[:, rows]
            azx0[d, r] = filters(1, r)[:, rows]
            for i, zz in enumerate(near):
                azm[0, i, d, r] = filters(2 * zz, r)[:, rows]
                azx1[i, d, r] = filters(2 * zz + 1, r)[:, rows]
        for i, zz in enumerate(far):
            rows = pl.ds(pl.multiple_of(day * part, part), part)
            azf[0, i, r] = filters(2 * zz, r)[:, rows]
            azx2[i, r] = filters(2 * zz + 1, r)[:, rows]

    pl.semaphore_wait(barrier, n - 1 + len(others))

    def remote(src, dst, send, recv, to_day, flip):
        return pltpu.make_async_remote_copy(
            src_ref=src,
            dst_ref=dst,
            send_sem=send,
            recv_sem=recv,
            device_id=(grp, to_day, me if flip is None else flipped(me, flip, n)),
            device_id_type=mesh_id,
        )

    swaps = [
        remote(xch.at[pl.ds(1, chips - 1)], mix.at[1], se.at[0], re.at[0], day, 1),
        remote(xch.at[0], xin.at[:, 1], se.at[1], re.at[1], day, 1),
        remote(azx0, azin.at[1], se.at[2], re.at[2], day, 1),
        remote(azx1, azm.at[1], se.at[3], re.at[3], day, 1),
    ]
    if far:
        swaps.append(remote(azx2, azf.at[1], se.at[4], re.at[4], day, 1))

    def direct(zz, cc):
        i = 2 * (zz - 1) + cc
        src = xch.at[zz, 0] if cc else mix.at[0, zz - 1, 0]
        return remote(src, xin.at[0, 2 * zz + cc], sd.at[i], rd.at[i], day, 2 * zz + cc)

    def step(k, zz):
        return remote(
            mix.at[:, zz - 1, k],
            xin.at[k, pl.ds(2 * zz, 2)],
            sz.at[k, zz - 1],
            rz.at[k, zz - 1],
            day,
            2 * zz,
        )

    def last(r, zz):
        return remote(
            mix.at[:, zz - 1, n - 1, r],
            xin.at[n - 1, pl.ds(2 * zz, 2), r],
            sz.at[n - 1 + r, zz - 1],
            rz.at[n - 1 + r, zz - 1],
            day,
            2 * zz,
        )

    def near_filter(i):
        zz = near[i]
        return remote(
            azm.at[:, i], azin.at[pl.ds(2 * zz, 2)], saz.at[zz - 1], raz.at[zz - 1], day, 2 * zz
        )

    def far_filter(i):
        zz = far[i]
        return remote(
            azf.at[:, i],
            azin.at[pl.ds(2 * zz, 2), day],
            saz.at[zz - 1],
            raz.at[zz - 1],
            day,
            2 * zz,
        )

    def pass_on(x):
        slab = azin.at[pl.ds(n // 2, n // 2), day]
        return remote(slab, slab, sf.at[x - 1], rf.at[x - 1], flipped(day, x, dates), None)

    swaps[0].start()
    swaps[1].start()
    for zz in range(chips - 1, 0, -1):
        for cc in range(2):
            direct(zz, cc).start()
    for swap in swaps[2:]:
        swap.start()
    swaps[0].wait_recv()
    for zz in range(chips - 1, 0, -1):
        step(1, zz).start()
    for swap in swaps[3:]:
        swap.wait_recv()
    for i in range(len(far)):
        far_filter(i).start()
    for i in range(len(near)):
        near_filter(i).start()

    def start_step(k, _):
        for zz in range(chips - 1, 0, -1):
            step(k, zz).start()
        return 0

    lax.fori_loop(2, n - 1, start_step, 0)
    for r in range(most):
        for zz in range(chips - 1, 0, -1):
            last(r, zz).start()

    held = lax.fori_loop(0, n, entries, (jnp.int32(total),) * capacity)
    for q in range(capacity):
        entry_ref[q] = held[q]
    fil[total] = jnp.zeros_like(fil[total])

    for load in loads[5:]:
        load.wait()

    joined = 0

    def copy_y(e, count):
        span = pl.ds(e, count)
        return remote(inbox.at[span], ybox.at[span], sy.at[e], ry.at[e], ydst, None)

    def copy_x(e, source, to, count):
        span = pl.ds(e, count)
        return remote(source.at[span], xbox.at[span], sx.at[e], rx.at[e], to, None)

    def focus(k, picks):
        columns = []
        filt = []
        for r in picks:
            pieces = [
                xin[k, flipped(me, s, n), r, c] for c in range(2) for s in range(n)
            ]
            columns.append(jnp.concatenate(pieces, axis=0))
            filt.append(
                [
                    jnp.concatenate([azin[k, d, r, c] for d in range(parts)], axis=0)
                    for c in range(2)
                ]
            )
        doppler = mm(pf_ref[...], jnp.concatenate(columns, axis=1))
        are = jnp.concatenate([f[0] for f in filt], axis=1).astype(F32)
        aim = jnp.concatenate([f[1] for f in filt], axis=1).astype(F32)
        dre = doppler[:wide]
        dim = doppler[wide:]
        shaped = jnp.concatenate([dre * are - dim * aim, dre * aim + dim * are], axis=0).astype(BF)
        image = mm(pb_ref[...], shaped).astype(BF)
        for i, r in enumerate(picks):
            e = k * most + r
            block = [
                jnp.concatenate(
                    [
                        image[c * wide + y * BLK : c * wide + (y + 1) * BLK, i * BLK : (i + 1) * BLK]
                        for c in range(2)
                    ],
                    axis=1,
                )
                for y in range(rows_of)
            ]
            if rows_of > 1:
                for y in range(rows_of):
                    img[i, y] = block[y]
                block = [img[i, row_ref[e]]]
            inbox[e] = mm(kt_ref[kind_ref[e]], block[0]).astype(BF)

    def stage_a(k):
        @pl.when(k == 0)
        def _():
            swaps[1].wait_recv()
            for zz in range(1, chips):
                for cc in range(2):
                    direct(zz, cc).wait_recv()

        @pl.when(k > 0)
        def _():
            for zz in range(1, chips):
                step(k, zz).wait_recv()

        @pl.when(k == 1)
        def _():
            swaps[2].wait_recv()

        for i, zz in enumerate(near):

            @pl.when(k == 2 * zz)
            def _():
                near_filter(i).wait_recv()

        if far:

            @pl.when(k == n // 2)
            def _():
                for x in range(1, dates):
                    pass_on(x).wait_recv()

        focus(k, range(most))

        def send(e, count):
            copy_y(e, count).start()
            if relay:

                @pl.when(parity == 1)
                def _():
                    copy_x(e, inbox, xdst, count).start()
            else:
                copy_x(e, inbox, xdst, count).start()

        each(k, range(most), send)

    def each(k, picks, act):
        for r in picks:

            @pl.when((k < joined) & (r == 0))
            def _():
                act(k * most, most)

            @pl.when(k >= joined)
            def _():
                act(k * most + r, 1)

    def stage_b(k, r):
        def onward(e, count):
            copy_y(e, count).wait_recv()
            if relay:

                @pl.when(parity == 0)
                def _():
                    copy_x(e, ybox, xdst, count).start()

        each(k, [r], onward)

    def patches(at):
        own = inbox[at].astype(F32)
        ore = own[:, :BLK]
        oim = own[:, BLK:]
        tops = []
        lows = []
        for box in (xbox, ybox):
            oth = box[at].astype(F32)
            tre = oth[:, :BLK]
            tim = oth[:, BLK:]
            tops.append(ore * tre + oim * tim)
            lows.append(oim * tre - ore * tim)
        pair = jnp.concatenate(
            [jnp.concatenate(tops, axis=1), jnp.concatenate(lows, axis=1)], axis=0
        ).astype(BF)

        def turned(x):
            return jnp.concatenate(
                [
                    jnp.concatenate([x[:BLK, :BLK], x[BLK:, :BLK]], axis=1),
                    jnp.concatenate([x[:BLK, BLK:], x[BLK:, BLK:]], axis=1),
                ],
                axis=0,
            )

        rows = mm(gfl_ref[...], pair).astype(BF)
        spectrum = mm(turned(rows), gfr_ref[...])
        weighted = []
        for x in range(2):
            spec = spectrum[x * BLK : (x + 1) * BLK]
            sre = spec[:, :BLK]
            sim = spec[:, BLK:]
            power = sre * sre + sim * sim
            line = power + pltpu.roll(power, 1, 1) + pltpu.roll(power, BLK - 1, 1)
            smooth = (line + pltpu.roll(line, 1, 0) + pltpu.roll(line, BLK - 1, 0)) * (1.0 / 9.0)
            level = jnp.sum(jnp.sum(smooth, axis=0, keepdims=True), axis=1, keepdims=True)
            level = level * (1.0 / (BLK * BLK)) + 1e-06
            weight = lax.rsqrt(lax.rsqrt(smooth * (1.0 / level)))
            weighted.append(jnp.concatenate([sre * weight, sim * weight], axis=1))
        weighted = jnp.concatenate(weighted, axis=0).astype(BF)
        back = mm(gbl_ref[...], turned(weighted)).astype(BF)
        done = mm(turned(back), gbr_ref[...]).astype(BF)
        for x in range(2):
            for c in range(2):
                fil[at, x, c] = done[x * BLK : (x + 1) * BLK, c * BLK : (c + 1) * BLK]

    def stage_c(k, r):
        each(k, [r], lambda e, count: copy_x(e, inbox, xdst, count).wait_recv())
        patches(k * most + r)

    def pace(kb, kc):
        def one(r, _):
            @pl.when(kb >= 0)
            def _():
                stage_b(kb, r)

            @pl.when(kc >= 0)
            def _():
                stage_c(kc, r)

            return 0

        lax.fori_loop(0, most, one, 0)

    lag = 3

    def main(t, _):
        stage_a(t)
        pace(t - 1, t - lag)
        if far:

            @pl.when(t == 1)
            def _():
                for i in range(len(far)):
                    far_filter(i).wait_recv()
                for x in range(1, dates):
                    pass_on(x).start()

        return 0

    lax.fori_loop(0, n - 1, main, 0)
    for r in range(most):
        for zz in range(1, chips):
            last(r, zz).wait_recv()
        focus(n - 1, [r])
        e = (n - 1) * most + r
        copy_y(e, 1).start()
        copy_x(e, inbox, xnext, 1).start()
    pace(n - 2, n - 1 - lag)

    def closing(i, _):
        k = n - lag + i // most
        r = lax.rem(i, most)

        @pl.when(k == n - 1)
        def _():
            copy_y(k * most + r, 1).wait_recv()

        stage_c(k, r)
        return 0

    lax.fori_loop(0, lag * most, closing, 0)

    def sent(e, count):
        copy_y(e, count).wait_send()
        copy_x(e, inbox, xdst, count).wait_send()

    def drain(k, _):
        each(k, range(most), sent)
        return 0

    for swap in swaps:
        swap.wait_send()
    for zz in range(1, chips):
        for cc in range(2):
            direct(zz, cc).wait_send()
        for r in range(most):
            last(r, zz).wait_send()

    def drain_step(k, _):
        for zz in range(1, chips):
            step(k, zz).wait_send()
        return 0

    lax.fori_loop(1, n - 1, drain_step, 0)
    for i in range(len(near)):
        near_filter(i).wait_send()
    for i in range(len(far)):
        far_filter(i).wait_send()
    if far:
        for x in range(1, dates):
            pass_on(x).wait_send()
    lax.fori_loop(0, n, drain, 0)


def place(capacity, entry_ref, fil, out_ref, sems):
    def copy(q):
        return pltpu.make_async_copy(fil.at[entry_ref[q]], out_ref.at[q], sems.at[q])

    for q in range(capacity):
        copy(q).start()
    for q in range(capacity):
        copy(q).wait()


def body(dates, echo_spectra, range_reference, azimuth_reference, block_owner, block_slot, kernel_index):
    n = lax.axis_size("shard")
    per = block_owner.shape[1] // n
    most = max(2, 2 * per // n)
    capacity = min(2 * per, n * most)
    echo = echo_spectra[0]
    pulses, rng = echo.shape[1:]
    inner = rng // BLK
    mine = rng // BLK // n
    wide = pulses * n
    chips = n // 2
    relay = dates == 4
    parts = dates if relay else 1
    part = wide // parts
    near = (chips // 2 if relay else chips) - 1
    far = chips - 1 - near
    tables = [
        first_table(rng),
        twiddle_table(rng),
        left_table(inner, 1),
        left_table(wide, -1),
        left_table(wide, 1),
        kernel_table(),
        left_table(BLK, -1),
        right_table(BLK, -1),
        left_table(BLK, 1),
        right_table(BLK, 1),
    ]
    smem = pl.BlockSpec(memory_space=pltpu.SMEM)
    hbm = pl.BlockSpec(memory_space=pl.ANY)
    vmem = pl.BlockSpec(memory_space=pltpu.VMEM)
    total = n * most
    box = pltpu.VMEM((total, BLK, 2 * BLK), BF)
    grant = min(60 * 1024 * 1024, 63 * 2**20 - (total + 2) * 4 * BLK * BLK * 2)
    dma = pltpu.SemaphoreType.DMA
    tables = [jnp.asarray(t) for t in tables]
    operands = [block_owner, block_slot, kernel_index, echo, range_reference, azimuth_reference]
    operands += tables
    held = [echo, range_reference] + tables
    filtered, entry = pl.pallas_call(
        functools.partial(kernel, n, dates, most, capacity),
        out_shape=(
            pltpu.VMEM((total + 1, 2, 2, BLK, BLK), BF),
            jax.ShapeDtypeStruct((capacity,), jnp.int32),
        ),
        in_specs=[smem] * 3 + [hbm] * 13,
        out_specs=(vmem, smem),
        scratch_shapes=[pltpu.VMEM(a.shape, a.dtype) for a in held]
        + [
            pltpu.VMEM((mine, 2, wide, BLK), BF),
            pltpu.SMEM((n * total,), jnp.int32),
            pltpu.SMEM((total,), jnp.int32),
            pltpu.SMEM((total,), jnp.int32),
            pltpu.VMEM((pulses * inner, 2 * BLK), BF),
            pltpu.VMEM((2, pulses, rng // BLK, BLK), F32),
            pltpu.VMEM((2, rng // BLK, pulses, BLK), BF),
            pltpu.VMEM((2, chips - 1, n, most, 2, pulses, BLK), BF),
            pltpu.VMEM((chips, n, most, 2, pulses, BLK), BF),
            pltpu.VMEM((n, n, most, 2, pulses, BLK), BF),
            pltpu.VMEM((n, parts, most, 2, part, BLK), BF),
            pltpu.VMEM((2, near, parts, most, 2, part, BLK), BF),
            pltpu.VMEM((2, max(far, 1), most, 2, part, BLK), BF),
            pltpu.VMEM((parts, most, 2, part, BLK), BF),
            pltpu.VMEM((near, parts, most, 2, part, BLK), BF),
            pltpu.VMEM((max(far, 1), most, 2, part, BLK), BF),
            pltpu.VMEM((most, wide // BLK, BLK, 2 * BLK), BF),
            box,
            box,
            box,
            dma((len(held),)),
            dma((mine,)),
            *[dma((5,))] * 2,
            *[dma((2 * (chips - 1),))] * 2,
            *[dma((n - 1 + most, chips - 1))] * 2,
            *[dma((chips - 1,))] * 2,
            *[dma((dates - 1,))] * 2,
            *[dma((total,))] * 4,
        ],
        compiler_params=pltpu.CompilerParams(
            collective_id=0, has_side_effects=True, vmem_limit_bytes=grant
        ),
    )(
        *operands
    )
    out = pl.pallas_call(
        functools.partial(place, capacity),
        out_shape=jax.ShapeDtypeStruct((capacity, 2, 2, BLK, BLK), BF),
        in_specs=[smem, vmem],
        out_specs=hbm,
        scratch_shapes=[dma((capacity,))],
        compiler_params=pltpu.CompilerParams(vmem_limit_bytes=grant),
    )(entry, pltpu.with_memory_space_constraint(filtered, pltpu.VMEM))
    return out[None]


def solution(mesh):
    in_specs = (
        P(("grp", "date"), None, "shard", None),
        P(),
        P(None, None, "shard"),
        P(("grp", "date"), None),
        P(("grp", "date"), None),
        P(("grp", "date"), None),
    )
    out_specs = P(("grp", "date"), "shard", None, None, None, None)
    return jax.shard_map(
        functools.partial(body, mesh.shape["date"]),
        mesh=mesh,
        in_specs=in_specs,
        out_specs=out_specs,
        check_vma=False,
    )
```

```python
import functools
import math

import jax
import jax.numpy as jnp
import ml_dtypes
import numpy as np
from jax import lax
from jax.experimental import pallas as pl
from jax.experimental.pallas import tpu as pltpu
from jax.sharding import PartitionSpec as P

BLK = 128
NSUB = 8
WORD = 4
BF = jnp.bfloat16
F32 = jnp.float32


def dft_parts(size, sign):
    index = np.arange(size)
    angle = 2.0 * math.pi / size * (index[:, None] * index[None, :] % size)
    scale = 1.0 / math.sqrt(size)
    return np.cos(angle) * scale, sign * np.sin(angle) * scale


def left_table(size, sign):
    cosine, sine = dft_parts(size, sign)
    return np.block([[cosine, -sine], [sine, cosine]]).astype(ml_dtypes.bfloat16)


def right_table(size, sign):
    return np.ascontiguousarray(left_table(size, sign).T)


def first_table(rng):
    outer, inner = BLK, rng // BLK
    low = outer * BLK // rng
    cosine, sine = dft_parts(outer, 1)
    full = np.stack([np.stack([cosine, sine], 1), np.stack([-sine, cosine], 1)])
    full = full.reshape(2, outer // low, low, 2 * outer)
    return np.transpose(full, (2, 0, 1, 3)).reshape(2 * outer, 2 * outer).astype(ml_dtypes.bfloat16)


def twiddle_table(rng):
    inner = rng // BLK
    phase = np.arange(inner)[:, None] * np.arange(BLK)[None, :] % rng
    angle = 2.0 * math.pi / rng * phase
    return np.stack([np.cos(angle), np.sin(angle)]).astype(np.float32)


def kernel_table():
    offset = (np.arange(NSUB) + 0.5) / NSUB
    cells = np.arange(BLK)
    dist = cells[None, None, :] - cells[None, :, None] - offset[:, None, None]
    window = np.where(np.abs(dist) < 4.0, 0.5 + 0.5 * np.cos(math.pi * dist / 4.0), 0.0)
    return (np.sinc(dist) * window).astype(ml_dtypes.bfloat16)


def flipped(a, b, n):
    total = 0
    bit = 1
    while bit < n:
        total = total + (a // bit + b // bit) % 2 * bit
        bit *= 2
    return total


def mm(left, right):
    return jnp.dot(left, right, preferred_element_type=F32)


def kernel(
    n,
    dates,
    most,
    capacity,
    owner_ref,
    slot_ref,
    kinds_ref,
    echo_hbm,
    rref_hbm,
    aref_hbm,
    t1_hbm,
    tw_hbm,
    w2_hbm,
    pf_hbm,
    pb_hbm,
    kt_hbm,
    gfl_hbm,
    gfr_hbm,
    gbl_hbm,
    gbr_hbm,
    fil,
    entry_out,
    entry_ref,
    sl,
    echo_ref,
    rref_ref,
    t1_ref,
    tw_ref,
    w2_ref,
    pf_ref,
    pb_ref,
    kt_ref,
    gfl_ref,
    gfr_ref,
    gbl_ref,
    gbr_ref,
    ats,
    tile_ref,
    kind_ref,
    row_ref,
    lhs,
    mat,
    snd,
    mix,
    xch,
    xin,
    azin,
    azm,
    azf,
    azx0,
    azx1,
    azx2,
    img,
    inbox,
    ybox,
    xbox,
    si,
    sa,
    se,
    re,
    sd,
    rd,
    sz,
    rz,
    saz,
    raz,
    sf,
    rf,
    sy,
    ry,
    sx,
    rx,
):
    me = lax.axis_index("shard")
    day = lax.axis_index("date")
    grp = lax.axis_index("grp")
    relay = dates == 4
    parity = lax.rem(day, 2)
    ydst = lax.rem(day + dates - 2, dates)
    xnext = lax.rem(day + dates - 1, dates)
    xdst = day + 1 - 2 * parity if relay else xnext
    mesh_id = pl.DeviceIdType.MESH

    barrier = pltpu.get_barrier_semaphore()

    def greet(k, _):
        pl.semaphore_signal(
            barrier, inc=1, device_id=(grp, day, flipped(me, k, n)), device_id_type=mesh_id
        )
        return 0

    lax.fori_loop(1, n, greet, 0)
    if relay:
        others = [flipped(day, x, dates) for x in range(1, dates)]
    else:
        others = [lax.rem(day + 2, dates), lax.rem(day + 1, dates)]
    for other in others:
        pl.semaphore_signal(barrier, inc=1, device_id=(grp, other, me), device_id_type=mesh_id)

    pulses = echo_ref.shape[1]
    rng = echo_ref.shape[2]
    tiles = rng // BLK
    inner = rng // BLK
    mine = tiles // n
    wide = n * pulses
    rows_of = wide // BLK
    chips = n // 2
    total = n * most
    per = owner_ref.shape[1] // n
    parts = azin.shape[1]
    part = wide // parts
    near = list(range(1, chips // 2 if relay else chips))
    far = list(range(chips // 2, chips)) if relay else []

    loads = [
        pltpu.make_async_copy(a, b, si.at[i])
        for i, (a, b) in enumerate(
            [
                (echo_hbm, echo_ref),
                (rref_hbm, rref_ref),
                (t1_hbm, t1_ref),
                (tw_hbm, tw_ref),
                (w2_hbm, w2_ref),
                (pf_hbm, pf_ref),
                (pb_hbm, pb_ref),
                (kt_hbm, kt_ref),
                (gfl_hbm, gfl_ref),
                (gfr_hbm, gfr_ref),
                (gbl_hbm, gbl_ref),
                (gbr_hbm, gbr_ref),
            ]
        )
    ]
    slabs = [
        pltpu.make_async_copy(aref_hbm.at[:, :, pl.ds(t * BLK, BLK)], ats.at[t], sa.at[t])
        for t in range(mine)
    ]
    for load in loads[:5] + slabs + loads[5:]:
        load.start()

    bits = 32 // WORD
    words = (n + bits - 1) // bits

    def sources(g, _):
        packed = [[jnp.int32(0)] * most for _ in range(words)]
        for b in range(per):
            owner = owner_ref[0, g * per + b]
            for w in range(words):
                shift = (owner - w * bits) * WORD
                live = None
                if words > 1:
                    live = owner // bits == w
                    shift = jnp.where(live, shift, 0)
                for r in range(most):
                    empty = ((packed[w][r] >> shift) & (2**WORD - 1)) == 0
                    put = empty if live is None else live & empty
                    packed[w][r] = packed[w][r] | jnp.where(put, (b + 1) << shift, 0)
                    live = ~empty if live is None else live & ~empty
        for w in range(words):
            for x in range(w * bits, min(n, (w + 1) * bits)):
                flip = flipped(me, x, n)
                for r in range(most):
                    found = (packed[w][r] >> ((x - w * bits) * WORD)) & (2**WORD - 1)
                    found = jnp.maximum(found - 1, 0)
                    tile_ref[(flip * n + flipped(g, x, n)) * most + r] = g * mine + lax.rem(found, mine)
        return 0

    lax.fori_loop(0, n, sources, 0)

    def entries(t, held):
        held = list(held)
        at = flipped(me, t, n) * most
        found = [jnp.int32(0)] * most
        seen = jnp.int32(0)
        for b in range(per):
            named = owner_ref[0, t * per + b] == me
            for r in range(most):
                found[r] = jnp.where(named & (seen == r), b, found[r])
            seen = seen + named.astype(jnp.int32)
        for r in range(most):
            row_ref[at + r] = found[r] // mine
            kind_ref[at + r] = kinds_ref[0, t * per + found[r]]
        for b in range(per):
            named = owner_ref[0, t * per + b] == me
            slot = jnp.where(named, slot_ref[0, t * per + b], -1)
            for q in range(capacity):
                held[q] = jnp.where(slot == q, at, held[q])
            at = at + named.astype(jnp.int32)
        return tuple(held)

    for load in loads[:5]:
        load.wait()
    real = echo_ref[0].astype(F32)
    imag = echo_ref[1].astype(F32)
    rre = rref_ref[0:1, :]
    rim = rref_ref[1:2, :]
    mat[0] = (real * rre + imag * rim).reshape(pulses, tiles, BLK)
    mat[1] = (imag * rre - real * rim).reshape(pulses, tiles, BLK)

    for p in range(pulses):
        both = jnp.concatenate([mat[0, p], mat[1, p]], axis=0).T
        low = BLK // inner
        pieces = [both[x * inner : (x + 1) * inner] for x in range(low)]
        lhs[p * inner : (p + 1) * inner, :] = jnp.concatenate(pieces, axis=1).astype(BF)

    twc = tw_ref[0]
    tws = tw_ref[1]
    group = 4
    for g in range(0, pulses, group):
        section = mm(lhs[g * inner : (g + group) * inner, :], t1_ref[...])
        rights = []
        for p in range(group):
            sre = section[p * inner : (p + 1) * inner, :BLK]
            sim = section[p * inner : (p + 1) * inner, BLK:]
            rights.append(
                jnp.concatenate([sre * twc - sim * tws, sre * tws + sim * twc], axis=0).astype(BF)
            )
        second = mm(w2_ref[...], jnp.concatenate(rights, axis=1))
        for p in range(group):
            mat[:, g + p] = second[:, p * BLK : (p + 1) * BLK].reshape(2, tiles, BLK)
    for c in range(2):
        snd[c] = jnp.swapaxes(mat[c], 0, 1).astype(BF)

    def gather(k, _):
        for zz in range(chips):
            for cc in range(2):
                for r in range(most):
                    piece = snd[:, tile_ref[((2 * zz + cc) * n + k) * most + r]]
                    if cc:
                        xch[zz, k, r] = piece
                    elif zz:
                        mix[0, zz - 1, k, r] = piece
                    else:
                        xin[k, 0, r] = piece
        return 0

    lax.fori_loop(0, n, gather, 0)

    for slab in slabs:
        slab.wait()

    def filters(j, r):
        return ats.at[tile_ref[(j * n + j) * most + r] - me * mine]

    for r in range(most):
        for d in range(parts):
            rows = slice(d * part, (d + 1) * part)
            azin[0, d, r] = filters(0, r)[:, rows]
            azx0[d, r] = filters(1, r)[:, rows]
            for i, zz in enumerate(near):
                azm[0, i, d, r] = filters(2 * zz, r)[:, rows]
                azx1[i, d, r] = filters(2 * zz + 1, r)[:, rows]
        for i, zz in enumerate(far):
            rows = pl.ds(pl.multiple_of(day * part, part), part)
            azf[0, i, r] = filters(2 * zz, r)[:, rows]
            azx2[i, r] = filters(2 * zz + 1, r)[:, rows]

    pl.semaphore_wait(barrier, n - 1 + len(others))

    def remote(src, dst, send, recv, to_day, flip):
        return pltpu.make_async_remote_copy(
            src_ref=src,
            dst_ref=dst,
            send_sem=send,
            recv_sem=recv,
            device_id=(grp, to_day, me if flip is None else flipped(me, flip, n)),
            device_id_type=mesh_id,
        )

    swaps = [
        remote(xch.at[pl.ds(1, chips - 1)], mix.at[1], se.at[0], re.at[0], day, 1),
        remote(xch.at[0], xin.at[:, 1], se.at[1], re.at[1], day, 1),
        remote(azx0, azin.at[1], se.at[2], re.at[2], day, 1),
        remote(azx1, azm.at[1], se.at[3], re.at[3], day, 1),
    ]
    if far:
        swaps.append(remote(azx2, azf.at[1], se.at[4], re.at[4], day, 1))

    def direct(zz, cc):
        i = 2 * (zz - 1) + cc
        src = xch.at[zz, 0] if cc else mix.at[0, zz - 1, 0]
        return remote(src, xin.at[0, 2 * zz + cc], sd.at[i], rd.at[i], day, 2 * zz + cc)

    def step(k, zz):
        return remote(
            mix.at[:, zz - 1, k],
            xin.at[k, pl.ds(2 * zz, 2)],
            sz.at[k, zz - 1],
            rz.at[k, zz - 1],
            day,
            2 * zz,
        )

    def last(r, zz):
        return remote(
            mix.at[:, zz - 1, n - 1, r],
            xin.at[n - 1, pl.ds(2 * zz, 2), r],
            sz.at[n - 1 + r, zz - 1],
            rz.at[n - 1 + r, zz - 1],
            day,
            2 * zz,
        )

    def near_filter(i):
        zz = near[i]
        return remote(
            azm.at[:, i], azin.at[pl.ds(2 * zz, 2)], saz.at[zz - 1], raz.at[zz - 1], day, 2 * zz
        )

    def far_filter(i):
        zz = far[i]
        return remote(
            azf.at[:, i],
            azin.at[pl.ds(2 * zz, 2), day],
            saz.at[zz - 1],
            raz.at[zz - 1],
            day,
            2 * zz,
        )

    def pass_on(x):
        slab = azin.at[pl.ds(n // 2, n // 2), day]
        return remote(slab, slab, sf.at[x - 1], rf.at[x - 1], flipped(day, x, dates), None)

    def pass_far(x, held):
        half = azin.at[pl.ds(n // 2 + (2 - x) * (n // 4), n // 4), held]
        return remote(half, half, sf.at[x + 1], rf.at[x + 1], flipped(day, x, dates), None)

    for swap in [swaps[1]] + swaps[4:] + swaps[:1]:
        swap.start()
    for zz in range(chips - 1, 0, -1):
        for cc in range(2):
            direct(zz, cc).start()
    for swap in swaps[2:4]:
        swap.start()
    for swap in swaps[4:]:
        swap.wait_recv()
    for i in range(len(far)):
        far_filter(i).start()
    swaps[0].wait_recv()
    for zz in range(chips - 1, 0, -1):
        step(1, zz).start()
    swaps[3].wait_recv()
    for i in range(len(near)):
        near_filter(i).start()

    def start_step(k, _):
        for zz in range(chips - 1, 0, -1):
            step(k, zz).start()
        return 0

    lax.fori_loop(2, n - 1, start_step, 0)
    for r in range(most):
        for zz in range(chips - 1, 0, -1):
            last(r, zz).start()

    held = lax.fori_loop(0, n, entries, (jnp.int32(total),) * capacity)
    for q in range(capacity):
        entry_ref[q] = held[q]
    list_copy = pltpu.make_async_copy(entry_ref, entry_out, sl.at[0])
    list_copy.start()
    fil[total] = jnp.zeros_like(fil[total])

    for load in loads[5:]:
        load.wait()

    joined = 0

    def copy_y(e, count):
        span = pl.ds(e, count)
        return remote(inbox.at[span], ybox.at[span], sy.at[e], ry.at[e], ydst, None)

    def copy_x(e, source, to, count):
        span = pl.ds(e, count)
        return remote(source.at[span], xbox.at[span], sx.at[e], rx.at[e], to, None)

    def focus(k, picks):
        columns = []
        filt = []
        for r in picks:
            pieces = [
                xin[k, flipped(me, s, n), r, c] for c in range(2) for s in range(n)
            ]
            columns.append(jnp.concatenate(pieces, axis=0))
            filt.append(
                [
                    jnp.concatenate([azin[k, d, r, c] for d in range(parts)], axis=0)
                    for c in range(2)
                ]
            )
        doppler = mm(pf_ref[...], jnp.concatenate(columns, axis=1))
        are = jnp.concatenate([f[0] for f in filt], axis=1).astype(F32)
        aim = jnp.concatenate([f[1] for f in filt], axis=1).astype(F32)
        dre = doppler[:wide]
        dim = doppler[wide:]
        shaped = jnp.concatenate([dre * are - dim * aim, dre * aim + dim * are], axis=0).astype(BF)
        image = mm(pb_ref[...], shaped).astype(BF)
        for i, r in enumerate(picks):
            e = k * most + r
            block = [
                jnp.concatenate(
                    [
                        image[c * wide + y * BLK : c * wide + (y + 1) * BLK, i * BLK : (i + 1) * BLK]
                        for c in range(2)
                    ],
                    axis=1,
                )
                for y in range(rows_of)
            ]
            if rows_of > 1:
                for y in range(rows_of):
                    img[i, y] = block[y]
                block = [img[i, row_ref[e]]]
            inbox[e] = mm(kt_ref[kind_ref[e]], block[0]).astype(BF)

    def stage_a(k):
        @pl.when(k == 0)
        def _():
            swaps[1].wait_recv()
            for zz in range(1, chips):
                for cc in range(2):
                    direct(zz, cc).wait_recv()

        @pl.when(k > 0)
        def _():
            for zz in range(1, chips):
                step(k, zz).wait_recv()

        @pl.when(k == 1)
        def _():
            swaps[2].wait_recv()

        for i, zz in enumerate(near):

            @pl.when(k == 2 * zz)
            def _():
                near_filter(i).wait_recv()

        if far:

            @pl.when(k == n // 2)
            def _():
                for x in (1, 2):
                    pass_far(x, flipped(day, 3, dates)).wait_recv()

        focus(k, range(most))

        def send(e, count):
            copy_y(e, count).start()
            if relay:

                @pl.when(parity == 1)
                def _():
                    copy_x(e, inbox, xdst, count).start()
            else:
                copy_x(e, inbox, xdst, count).start()

        each(k, range(most), send)

    def each(k, picks, act):
        for r in picks:

            @pl.when((k < joined) & (r == 0))
            def _():
                act(k * most, most)

            @pl.when(k >= joined)
            def _():
                act(k * most + r, 1)

    def stage_b(k, r):
        def onward(e, count):
            copy_y(e, count).wait_recv()
            if relay:

                @pl.when(parity == 0)
                def _():
                    copy_x(e, ybox, xdst, count).start()

        each(k, [r], onward)

    def patches(at):
        own = inbox[at].astype(F32)
        ore = own[:, :BLK]
        oim = own[:, BLK:]
        tops = []
        lows = []
        for box in (xbox, ybox):
            oth = box[at].astype(F32)
            tre = oth[:, :BLK]
            tim = oth[:, BLK:]
            tops.append(ore * tre + oim * tim)
            lows.append(oim * tre - ore * tim)
        pair = jnp.concatenate(
            [jnp.concatenate(tops, axis=1), jnp.concatenate(lows, axis=1)], axis=0
        ).astype(BF)

        def turned(x):
            return jnp.concatenate(
                [
                    jnp.concatenate([x[:BLK, :BLK], x[BLK:, :BLK]], axis=1),
                    jnp.concatenate([x[:BLK, BLK:], x[BLK:, BLK:]], axis=1),
                ],
                axis=0,
            )

        rows = mm(gfl_ref[...], pair).astype(BF)
        spectrum = mm(turned(rows), gfr_ref[...])
        weighted = []
        for x in range(2):
            spec = spectrum[x * BLK : (x + 1) * BLK]
            sre = spec[:, :BLK]
            sim = spec[:, BLK:]
            power = sre * sre + sim * sim
            line = power + pltpu.roll(power, 1, 1) + pltpu.roll(power, BLK - 1, 1)
            smooth = (line + pltpu.roll(line, 1, 0) + pltpu.roll(line, BLK - 1, 0)) * (1.0 / 9.0)
            level = jnp.sum(jnp.sum(smooth, axis=0, keepdims=True), axis=1, keepdims=True)
            level = level * (1.0 / (BLK * BLK)) + 1e-06
            weight = lax.rsqrt(lax.rsqrt(smooth * (1.0 / level)))
            weighted.append(jnp.concatenate([sre * weight, sim * weight], axis=1))
        weighted = jnp.concatenate(weighted, axis=0).astype(BF)
        back = mm(gbl_ref[...], turned(weighted)).astype(BF)
        done = mm(turned(back), gbr_ref[...]).astype(BF)
        for x in range(2):
            for c in range(2):
                fil[at, x, c] = done[x * BLK : (x + 1) * BLK, c * BLK : (c + 1) * BLK]

    def stage_c(k, r):
        each(k, [r], lambda e, count: copy_x(e, inbox, xdst, count).wait_recv())
        patches(k * most + r)

    def pace(kb, kc):
        def one(r, _):
            @pl.when(kb >= 0)
            def _():
                stage_b(kb, r)

            @pl.when(kc >= 0)
            def _():
                stage_c(kc, r)

            return 0

        lax.fori_loop(0, most, one, 0)

    lag = 2

    def main(t, _):
        stage_a(t)
        pace(t - 1, t - lag)
        if far:

            @pl.when(t == 0)
            def _():
                for i in range(len(far)):
                    far_filter(i).wait_recv()
                for x in (1, 2):
                    pass_on(x).start()

            @pl.when(t == 1)
            def _():
                for x in (1, 2):
                    pass_on(3 - x).wait_recv()
                    pass_far(x, flipped(day, 3 - x, dates)).start()

        return 0

    lax.fori_loop(0, n - 1, main, 0)
    for r in range(most):
        for zz in range(1, chips):
            last(r, zz).wait_recv()
        focus(n - 1, [r])
        e = (n - 1) * most + r
        copy_y(e, 1).start()
        if r == most - 1:
            copy_x(e, inbox, xnext, 1).start()
        elif relay:

            @pl.when(parity == 1)
            def _():
                copy_x(e, inbox, xdst, 1).start()
        else:
            copy_x(e, inbox, xdst, 1).start()
    pace(n - 2, n - 1 - lag)
    for r in range(most - 1):
        stage_b(n - 1, r)

    def closing(i, _):
        k = n - lag + i // most
        r = lax.rem(i, most)

        @pl.when((k == n - 1) & (r == most - 1))
        def _():
            copy_y(k * most + r, 1).wait_recv()

        stage_c(k, r)
        return 0

    lax.fori_loop(0, lag * most, closing, 0)

    def sent(e, count):
        copy_y(e, count).wait_send()
        copy_x(e, inbox, xdst, count).wait_send()

    def drain(k, _):
        each(k, range(most), sent)
        return 0

    for swap in swaps:
        swap.wait_send()
    for zz in range(1, chips):
        for cc in range(2):
            direct(zz, cc).wait_send()
        for r in range(most):
            last(r, zz).wait_send()

    def drain_step(k, _):
        for zz in range(1, chips):
            step(k, zz).wait_send()
        return 0

    lax.fori_loop(1, n - 1, drain_step, 0)
    for i in range(len(near)):
        near_filter(i).wait_send()
    for i in range(len(far)):
        far_filter(i).wait_send()
    if far:
        for x in (1, 2):
            pass_on(x).wait_send()
            pass_far(x, flipped(day, 3 - x, dates)).wait_send()
    lax.fori_loop(0, n, drain, 0)
    list_copy.wait()


def place(capacity, entry_ref, fil, out_ref, sems):
    def copy(q):
        return pltpu.make_async_copy(fil.at[entry_ref[q]], out_ref.at[q], sems.at[q])

    for q in range(capacity):
        copy(q).start()
    for q in range(capacity):
        copy(q).wait()


def body(dates, echo_spectra, range_reference, azimuth_reference, block_owner, block_slot, kernel_index):
    n = lax.axis_size("shard")
    per = block_owner.shape[1] // n
    most = max(2, 2 * per // n)
    capacity = min(2 * per, n * most)
    echo = echo_spectra[0]
    pulses, rng = echo.shape[1:]
    inner = rng // BLK
    mine = rng // BLK // n
    wide = pulses * n
    chips = n // 2
    relay = dates == 4
    parts = dates if relay else 1
    part = wide // parts
    near = (chips // 2 if relay else chips) - 1
    far = chips - 1 - near
    tables = [
        first_table(rng),
        twiddle_table(rng),
        left_table(inner, 1),
        left_table(wide, -1),
        left_table(wide, 1),
        kernel_table(),
        left_table(BLK, -1),
        right_table(BLK, -1),
        left_table(BLK, 1),
        right_table(BLK, 1),
    ]
    smem = pl.BlockSpec(memory_space=pltpu.SMEM)
    hbm = pl.BlockSpec(memory_space=pl.ANY)
    vmem = pl.BlockSpec(memory_space=pltpu.VMEM)
    total = n * most
    box = pltpu.VMEM((total, BLK, 2 * BLK), BF)
    grant = min(60 * 1024 * 1024, 63 * 2**20 - (total + 2) * 4 * BLK * BLK * 2)
    dma = pltpu.SemaphoreType.DMA
    tables = [jnp.asarray(t) for t in tables]
    operands = [block_owner, block_slot, kernel_index, echo, range_reference, azimuth_reference]
    operands += tables
    held = [echo, range_reference] + tables
    filtered, entry = pl.pallas_call(
        functools.partial(kernel, n, dates, most, capacity),
        out_shape=(
            pltpu.VMEM((total + 1, 2, 2, BLK, BLK), BF),
            jax.ShapeDtypeStruct((capacity,), jnp.int32),
        ),
        in_specs=[smem] * 3 + [hbm] * 13,
        out_specs=(vmem, hbm),
        scratch_shapes=[pltpu.SMEM((capacity,), jnp.int32), dma((1,))]
        + [pltpu.VMEM(a.shape, a.dtype) for a in held]
        + [
            pltpu.VMEM((mine, 2, wide, BLK), BF),
            pltpu.SMEM((n * total,), jnp.int32),
            pltpu.SMEM((total,), jnp.int32),
            pltpu.SMEM((total,), jnp.int32),
            pltpu.VMEM((pulses * inner, 2 * BLK), BF),
            pltpu.VMEM((2, pulses, rng // BLK, BLK), F32),
            pltpu.VMEM((2, rng // BLK, pulses, BLK), BF),
            pltpu.VMEM((2, chips - 1, n, most, 2, pulses, BLK), BF),
            pltpu.VMEM((chips, n, most, 2, pulses, BLK), BF),
            pltpu.VMEM((n, n, most, 2, pulses, BLK), BF),
            pltpu.VMEM((n, parts, most, 2, part, BLK), BF),
            pltpu.VMEM((2, near, parts, most, 2, part, BLK), BF),
            pltpu.VMEM((2, max(far, 1), most, 2, part, BLK), BF),
            pltpu.VMEM((parts, most, 2, part, BLK), BF),
            pltpu.VMEM((near, parts, most, 2, part, BLK), BF),
            pltpu.VMEM((max(far, 1), most, 2, part, BLK), BF),
            pltpu.VMEM((most, wide // BLK, BLK, 2 * BLK), BF),
            box,
            box,
            box,
            dma((len(held),)),
            dma((mine,)),
            *[dma((5,))] * 2,
            *[dma((2 * (chips - 1),))] * 2,
            *[dma((n - 1 + most, chips - 1))] * 2,
            *[dma((chips - 1,))] * 2,
            *[dma((4,))] * 2,
            *[dma((total,))] * 4,
        ],
        compiler_params=pltpu.CompilerParams(
            collective_id=0, has_side_effects=True, vmem_limit_bytes=grant
        ),
    )(
        *operands
    )
    out = pl.pallas_call(
        functools.partial(place, capacity),
        out_shape=jax.ShapeDtypeStruct((capacity, 2, 2, BLK, BLK), BF),
        in_specs=[smem, vmem],
        out_specs=hbm,
        scratch_shapes=[dma((capacity,))],
        compiler_params=pltpu.CompilerParams(vmem_limit_bytes=grant),
    )(entry, pltpu.with_memory_space_constraint(filtered, pltpu.VMEM))
    return out[None]


def solution(mesh):
    in_specs = (
        P(("grp", "date"), None, "shard", None),
        P(),
        P(None, None, "shard"),
        P(("grp", "date"), None),
        P(("grp", "date"), None),
        P(("grp", "date"), None),
    )
    out_specs = P(("grp", "date"), "shard", None, None, None, None)
    return jax.shard_map(
        functools.partial(body, mesh.shape["date"]),
        mesh=mesh,
        in_specs=in_specs,
        out_specs=out_specs,
        check_vma=False,
    )
```

```python
import functools
import math

import jax
import jax.numpy as jnp
import ml_dtypes
import numpy as np
from jax import lax
from jax.experimental import pallas as pl
from jax.experimental.pallas import tpu as pltpu
from jax.sharding import PartitionSpec as P

BLK = 128
NSUB = 8
WORD = 4
BF = jnp.bfloat16
F32 = jnp.float32


def dft_parts(size, sign):
    index = np.arange(size)
    angle = 2.0 * math.pi / size * (index[:, None] * index[None, :] % size)
    scale = 1.0 / math.sqrt(size)
    return np.cos(angle) * scale, sign * np.sin(angle) * scale


def left_table(size, sign):
    cosine, sine = dft_parts(size, sign)
    return np.block([[cosine, -sine], [sine, cosine]]).astype(ml_dtypes.bfloat16)


def right_table(size, sign):
    return np.ascontiguousarray(left_table(size, sign).T)


def first_table(rng):
    outer, inner = BLK, rng // BLK
    low = outer * BLK // rng
    cosine, sine = dft_parts(outer, 1)
    full = np.stack([np.stack([cosine, sine], 1), np.stack([-sine, cosine], 1)])
    full = full.reshape(2, outer // low, low, 2 * outer)
    return np.transpose(full, (2, 0, 1, 3)).reshape(2 * outer, 2 * outer).astype(ml_dtypes.bfloat16)


def twiddle_table(rng):
    inner = rng // BLK
    phase = np.arange(inner)[:, None] * np.arange(BLK)[None, :] % rng
    angle = 2.0 * math.pi / rng * phase
    return np.stack([np.cos(angle), np.sin(angle)]).astype(np.float32)


def kernel_table():
    offset = (np.arange(NSUB) + 0.5) / NSUB
    cells = np.arange(BLK)
    dist = cells[None, None, :] - cells[None, :, None] - offset[:, None, None]
    window = np.where(np.abs(dist) < 4.0, 0.5 + 0.5 * np.cos(math.pi * dist / 4.0), 0.0)
    return (np.sinc(dist) * window).astype(ml_dtypes.bfloat16)


def flipped(a, b, n):
    total = 0
    bit = 1
    while bit < n:
        total = total + (a // bit + b // bit) % 2 * bit
        bit *= 2
    return total


def mm(left, right):
    return jnp.dot(left, right, preferred_element_type=F32)


def kernel(
    n,
    dates,
    most,
    capacity,
    owner_ref,
    slot_ref,
    kinds_ref,
    echo_hbm,
    rref_hbm,
    aref_hbm,
    t1_hbm,
    tw_hbm,
    w2_hbm,
    pf_hbm,
    pb_hbm,
    kt_hbm,
    gfl_hbm,
    gfr_hbm,
    gbl_hbm,
    gbr_hbm,
    fil,
    entry_out,
    entry_ref,
    sl,
    echo_ref,
    rref_ref,
    t1_ref,
    tw_ref,
    w2_ref,
    pf_ref,
    pb_ref,
    kt_ref,
    gfl_ref,
    gfr_ref,
    gbl_ref,
    gbr_ref,
    ats,
    tile_ref,
    kind_ref,
    row_ref,
    lhs,
    mat,
    snd,
    mix,
    xch,
    xin,
    azin,
    azm,
    azf,
    azx0,
    azx1,
    azx2,
    img,
    inbox,
    ybox,
    xbox,
    si,
    sa,
    se,
    re,
    sd,
    rd,
    sz,
    rz,
    saz,
    raz,
    sf,
    rf,
    sy,
    ry,
    sx,
    rx,
):
    me = lax.axis_index("shard")
    day = lax.axis_index("date")
    grp = lax.axis_index("grp")
    relay = dates == 4
    parity = lax.rem(day, 2)
    ydst = lax.rem(day + dates - 2, dates)
    xnext = lax.rem(day + dates - 1, dates)
    xdst = day + 1 - 2 * parity if relay else xnext
    mesh_id = pl.DeviceIdType.MESH

    barrier = pltpu.get_barrier_semaphore()

    def greet(k, _):
        pl.semaphore_signal(
            barrier, inc=1, device_id=(grp, day, flipped(me, k, n)), device_id_type=mesh_id
        )
        return 0

    lax.fori_loop(1, n, greet, 0)
    if relay:
        others = [flipped(day, x, dates) for x in range(1, dates)]
    else:
        others = [lax.rem(day + 2, dates), lax.rem(day + 1, dates)]
    for other in others:
        pl.semaphore_signal(barrier, inc=1, device_id=(grp, other, me), device_id_type=mesh_id)

    pulses = echo_ref.shape[1]
    rng = echo_ref.shape[2]
    tiles = rng // BLK
    inner = rng // BLK
    mine = tiles // n
    wide = n * pulses
    rows_of = wide // BLK
    chips = n // 2
    total = n * most
    per = owner_ref.shape[1] // n
    parts = azin.shape[1]
    part = wide // parts
    near = list(range(1, chips // 2 if relay else chips))
    far = list(range(chips // 2, chips)) if relay else []

    loads = [
        pltpu.make_async_copy(a, b, si.at[i])
        for i, (a, b) in enumerate(
            [
                (echo_hbm, echo_ref),
                (rref_hbm, rref_ref),
                (t1_hbm, t1_ref),
                (tw_hbm, tw_ref),
                (w2_hbm, w2_ref),
                (pf_hbm, pf_ref),
                (pb_hbm, pb_ref),
                (kt_hbm, kt_ref),
                (gfl_hbm, gfl_ref),
                (gfr_hbm, gfr_ref),
                (gbl_hbm, gbl_ref),
                (gbr_hbm, gbr_ref),
            ]
        )
    ]
    slabs = [
        pltpu.make_async_copy(aref_hbm.at[:, :, pl.ds(t * BLK, BLK)], ats.at[t], sa.at[t])
        for t in range(mine)
    ]
    for load in loads[:5] + slabs + loads[5:]:
        load.start()

    bits = 32 // WORD
    words = (n + bits - 1) // bits

    def sources(g, _):
        packed = [[jnp.int32(0)] * most for _ in range(words)]
        for b in range(per):
            owner = owner_ref[0, g * per + b]
            for w in range(words):
                shift = (owner - w * bits) * WORD
                live = None
                if words > 1:
                    live = owner // bits == w
                    shift = jnp.where(live, shift, 0)
                for r in range(most):
                    empty = ((packed[w][r] >> shift) & (2**WORD - 1)) == 0
                    put = empty if live is None else live & empty
                    packed[w][r] = packed[w][r] | jnp.where(put, (b + 1) << shift, 0)
                    live = ~empty if live is None else live & ~empty
        for w in range(words):
            for x in range(w * bits, min(n, (w + 1) * bits)):
                flip = flipped(me, x, n)
                for r in range(most):
                    found = (packed[w][r] >> ((x - w * bits) * WORD)) & (2**WORD - 1)
                    found = jnp.maximum(found - 1, 0)
                    tile_ref[(flip * n + flipped(g, x, n)) * most + r] = g * mine + lax.rem(found, mine)
        return 0

    lax.fori_loop(0, n, sources, 0)

    def entries(t, held):
        held = list(held)
        at = flipped(me, t, n) * most
        found = [jnp.int32(0)] * most
        seen = jnp.int32(0)
        for b in range(per):
            named = owner_ref[0, t * per + b] == me
            for r in range(most):
                found[r] = jnp.where(named & (seen == r), b, found[r])
            seen = seen + named.astype(jnp.int32)
        for r in range(most):
            row_ref[at + r] = found[r] // mine
            kind_ref[at + r] = kinds_ref[0, t * per + found[r]]
        for b in range(per):
            named = owner_ref[0, t * per + b] == me
            slot = jnp.where(named, slot_ref[0, t * per + b], -1)
            for q in range(capacity):
                held[q] = jnp.where(slot == q, at, held[q])
            at = at + named.astype(jnp.int32)
        return tuple(held)

    for load in loads[:5]:
        load.wait()
    real = echo_ref[0].astype(F32)
    imag = echo_ref[1].astype(F32)
    rre = rref_ref[0:1, :]
    rim = rref_ref[1:2, :]
    mat[0] = (real * rre + imag * rim).reshape(pulses, tiles, BLK)
    mat[1] = (imag * rre - real * rim).reshape(pulses, tiles, BLK)

    for p in range(pulses):
        both = jnp.concatenate([mat[0, p], mat[1, p]], axis=0).T
        low = BLK // inner
        pieces = [both[x * inner : (x + 1) * inner] for x in range(low)]
        lhs[p * inner : (p + 1) * inner, :] = jnp.concatenate(pieces, axis=1).astype(BF)

    twc = tw_ref[0]
    tws = tw_ref[1]
    group = 4
    for g in range(0, pulses, group):
        section = mm(lhs[g * inner : (g + group) * inner, :], t1_ref[...])
        rights = []
        for p in range(group):
            sre = section[p * inner : (p + 1) * inner, :BLK]
            sim = section[p * inner : (p + 1) * inner, BLK:]
            rights.append(
                jnp.concatenate([sre * twc - sim * tws, sre * tws + sim * twc], axis=0).astype(BF)
            )
        second = mm(w2_ref[...], jnp.concatenate(rights, axis=1))
        for p in range(group):
            mat[:, g + p] = second[:, p * BLK : (p + 1) * BLK].reshape(2, tiles, BLK)
    for c in range(2):
        snd[c] = jnp.swapaxes(mat[c], 0, 1).astype(BF)

    def gather(k, _):
        for zz in range(chips):
            for cc in range(2):
                for r in range(most):
                    piece = snd[:, tile_ref[((2 * zz + cc) * n + k) * most + r]]
                    if cc:
                        xch[zz, k, r] = piece
                    elif zz:
                        mix[0, zz - 1, k, r] = piece
                    else:
                        xin[0, k, r] = piece
        return 0

    gather(0, 0)

    for slab in slabs:
        slab.wait()

    def filters(j, r):
        return ats.at[tile_ref[(j * n + j) * most + r] - me * mine]

    for r in range(most):
        for i, zz in enumerate(far):
            rows = pl.ds(pl.multiple_of(day * part, part), part)
            azf[0, i, r] = filters(2 * zz, r)[:, rows]
            azx2[i, r] = filters(2 * zz + 1, r)[:, rows]

    pl.semaphore_wait(barrier, n - 1 + len(others))

    def remote(src, dst, send, recv, to_day, flip):
        return pltpu.make_async_remote_copy(
            src_ref=src,
            dst_ref=dst,
            send_sem=send,
            recv_sem=recv,
            device_id=(grp, to_day, me if flip is None else flipped(me, flip, n)),
            device_id_type=mesh_id,
        )

    swaps = [
        remote(xch.at[pl.ds(1, chips - 1)], mix.at[1], se.at[0], re.at[0], day, 1),
        remote(xch.at[0], xin.at[1], se.at[1], re.at[1], day, 1),
        remote(azx0, azin.at[1], se.at[2], re.at[2], day, 1),
        remote(azx1, azm.at[1], se.at[3], re.at[3], day, 1),
    ]
    if far:
        swaps.append(remote(azx2, azf.at[1], se.at[4], re.at[4], day, 1))

    def direct(zz, cc):
        i = 2 * (zz - 1) + cc
        src = xch.at[zz, 0] if cc else mix.at[0, zz - 1, 0]
        return remote(src, xin.at[2 * zz + cc, 0], sd.at[i], rd.at[i], day, 2 * zz + cc)

    def step(k, zz, count=1):
        span = pl.ds(k, count)
        return remote(
            mix.at[:, zz - 1, span],
            xin.at[pl.ds(2 * zz, 2), span],
            sz.at[k, zz - 1],
            rz.at[k, zz - 1],
            day,
            2 * zz,
        )

    def last(r, zz):
        return remote(
            mix.at[:, zz - 1, n - 1, r],
            xin.at[pl.ds(2 * zz, 2), n - 1, r],
            sz.at[n - 1 + r, zz - 1],
            rz.at[n - 1 + r, zz - 1],
            day,
            2 * zz,
        )

    def near_filter(i):
        zz = near[i]
        return remote(
            azm.at[:, i], azin.at[pl.ds(2 * zz, 2)], saz.at[zz - 1], raz.at[zz - 1], day, 2 * zz
        )

    def far_filter(i):
        zz = far[i]
        return remote(
            azf.at[:, i],
            azin.at[pl.ds(2 * zz, 2), day],
            saz.at[zz - 1],
            raz.at[zz - 1],
            day,
            2 * zz,
        )

    def pass_on(x):
        slab = azin.at[pl.ds(n // 2, n // 2), day]
        return remote(slab, slab, sf.at[x - 1], rf.at[x - 1], flipped(day, x, dates), None)

    def pass_far(x, held):
        half = azin.at[pl.ds(n // 2 + (2 - x) * (n // 4), n // 4), held]
        return remote(half, half, sf.at[x + 1], rf.at[x + 1], flipped(day, x, dates), None)

    for zz in range(chips - 1, 0, -1):
        for cc in range(2):
            direct(zz, cc).start()
    for swap in swaps[4:]:
        swap.start()
    lax.fori_loop(1, n, gather, 0)
    swaps[1].start()
    swaps[0].start()
    for r in range(most):
        for d in range(parts):
            rows = slice(d * part, (d + 1) * part)
            azin[0, d, r] = filters(0, r)[:, rows]
            azx0[d, r] = filters(1, r)[:, rows]
            for i, zz in enumerate(near):
                azm[0, i, d, r] = filters(2 * zz, r)[:, rows]
                azx1[i, d, r] = filters(2 * zz + 1, r)[:, rows]
    for swap in swaps[2:4]:
        swap.start()
    for swap in swaps[4:]:
        swap.wait_recv()
    for i in range(len(far)):
        far_filter(i).start()
    swaps[0].wait_recv()
    for zz in range(chips - 1, 0, -1):
        step(1, zz).start()
    swaps[3].wait_recv()
    for i in range(len(near)):
        near_filter(i).start()

    def start_step(k, _):
        for zz in range(chips - 1, 0, -1):
            step(k, zz).start()
        return 0

    lax.fori_loop(2, n - 1, start_step, 0)
    for r in range(most):
        for zz in range(chips - 1, 0, -1):
            last(r, zz).start()

    held = lax.fori_loop(0, n, entries, (jnp.int32(total),) * capacity)
    for q in range(capacity):
        entry_ref[q] = held[q]
    list_copy = pltpu.make_async_copy(entry_ref, entry_out, sl.at[0])
    list_copy.start()
    fil[total] = jnp.zeros_like(fil[total])

    for load in loads[5:]:
        load.wait()

    joined = 0

    def copy_y(e, count):
        span = pl.ds(e, count)
        return remote(inbox.at[span], ybox.at[span], sy.at[e], ry.at[e], ydst, None)

    def copy_x(e, source, to, count):
        span = pl.ds(e, count)
        return remote(source.at[span], xbox.at[span], sx.at[e], rx.at[e], to, None)

    def focus(k, picks):
        columns = []
        filt = []
        for r in picks:
            pieces = [
                xin[flipped(me, s, n), k, r, c] for c in range(2) for s in range(n)
            ]
            columns.append(jnp.concatenate(pieces, axis=0))
            filt.append(
                [
                    jnp.concatenate([azin[k, d, r, c] for d in range(parts)], axis=0)
                    for c in range(2)
                ]
            )
        doppler = mm(pf_ref[...], jnp.concatenate(columns, axis=1))
        are = jnp.concatenate([f[0] for f in filt], axis=1).astype(F32)
        aim = jnp.concatenate([f[1] for f in filt], axis=1).astype(F32)
        dre = doppler[:wide]
        dim = doppler[wide:]
        shaped = jnp.concatenate([dre * are - dim * aim, dre * aim + dim * are], axis=0).astype(BF)
        image = mm(pb_ref[...], shaped).astype(BF)
        for i, r in enumerate(picks):
            e = k * most + r
            block = [
                jnp.concatenate(
                    [
                        image[c * wide + y * BLK : c * wide + (y + 1) * BLK, i * BLK : (i + 1) * BLK]
                        for c in range(2)
                    ],
                    axis=1,
                )
                for y in range(rows_of)
            ]
            if rows_of > 1:
                for y in range(rows_of):
                    img[i, y] = block[y]
                block = [img[i, row_ref[e]]]
            inbox[e] = mm(kt_ref[kind_ref[e]], block[0]).astype(BF)

    def stage_a(k):
        @pl.when(k == 0)
        def _():
            swaps[1].wait_recv()
            for zz in range(1, chips):
                for cc in range(2):
                    direct(zz, cc).wait_recv()

        @pl.when(k > 0)
        def _():
            for zz in range(1, chips):
                step(k, zz).wait_recv()

        @pl.when(k == 1)
        def _():
            swaps[2].wait_recv()

        for i, zz in enumerate(near):

            @pl.when(k == 2 * zz)
            def _():
                near_filter(i).wait_recv()

        if far:

            @pl.when(k == n // 2)
            def _():
                for x in (1, 2):
                    pass_far(x, flipped(day, 3, dates)).wait_recv()

        focus(k, range(most))

        def send(e, count):
            copy_y(e, count).start()
            if relay:

                @pl.when(parity == 1)
                def _():
                    copy_x(e, inbox, xdst, count).start()
            else:
                copy_x(e, inbox, xdst, count).start()

        each(k, range(most), send)

    def each(k, picks, act):
        for r in picks:

            @pl.when((k < joined) & (r == 0))
            def _():
                act(k * most, most)

            @pl.when(k >= joined)
            def _():
                act(k * most + r, 1)

    def stage_b(k, r):
        def onward(e, count):
            copy_y(e, count).wait_recv()
            if relay:

                @pl.when(parity == 0)
                def _():
                    copy_x(e, ybox, xdst, count).start()

        each(k, [r], onward)

    def patches(at):
        own = inbox[at].astype(F32)
        ore = own[:, :BLK]
        oim = own[:, BLK:]
        tops = []
        lows = []
        for box in (xbox, ybox):
            oth = box[at].astype(F32)
            tre = oth[:, :BLK]
            tim = oth[:, BLK:]
            tops.append(ore * tre + oim * tim)
            lows.append(oim * tre - ore * tim)
        pair = jnp.concatenate(
            [jnp.concatenate(tops, axis=1), jnp.concatenate(lows, axis=1)], axis=0
        ).astype(BF)

        def turned(x):
            return jnp.concatenate(
                [
                    jnp.concatenate([x[:BLK, :BLK], x[BLK:, :BLK]], axis=1),
                    jnp.concatenate([x[:BLK, BLK:], x[BLK:, BLK:]], axis=1),
                ],
                axis=0,
            )

        rows = mm(gfl_ref[...], pair).astype(BF)
        spectrum = mm(turned(rows), gfr_ref[...])
        weighted = []
        for x in range(2):
            spec = spectrum[x * BLK : (x + 1) * BLK]
            sre = spec[:, :BLK]
            sim = spec[:, BLK:]
            power = sre * sre + sim * sim
            line = power + pltpu.roll(power, 1, 1) + pltpu.roll(power, BLK - 1, 1)
            smooth = line + pltpu.roll(line, 1, 0) + pltpu.roll(line, BLK - 1, 0)
            level = jnp.sum(jnp.sum(power, axis=0, keepdims=True), axis=1, keepdims=True)
            level = 9.0 * (level * (1.0 / (BLK * BLK)) + 1e-06)
            weight = lax.rsqrt(lax.rsqrt(smooth * (1.0 / level)))
            weighted.append(jnp.concatenate([sre * weight, sim * weight], axis=1))
        weighted = jnp.concatenate(weighted, axis=0).astype(BF)
        back = mm(gbl_ref[...], turned(weighted)).astype(BF)
        done = mm(turned(back), gbr_ref[...]).astype(BF)
        for x in range(2):
            for c in range(2):
                fil[at, x, c] = done[x * BLK : (x + 1) * BLK, c * BLK : (c + 1) * BLK]

    def stage_c(k, r):
        each(k, [r], lambda e, count: copy_x(e, inbox, xdst, count).wait_recv())
        patches(k * most + r)

    def pace(kb, kc):
        def one(r, _):
            @pl.when(kc >= 0)
            def _():
                stage_c(kc, r)

            @pl.when(kb >= 0)
            def _():
                stage_b(kb, r)

            return 0

        lax.fori_loop(0, most, one, 0)

    lag = 2

    def main(t, _):
        stage_a(t)
        pace(t - 1, t - lag)
        if far:

            @pl.when(t == 0)
            def _():
                for i in range(len(far)):
                    far_filter(i).wait_recv()
                for x in (1, 2):
                    pass_on(x).start()

            @pl.when(t == 1)
            def _():
                for x in (1, 2):
                    pass_on(3 - x).wait_recv()
                    pass_far(x, flipped(day, 3 - x, dates)).start()

        return 0

    lax.fori_loop(0, n - 1, main, 0)
    for r in range(most):
        for zz in range(1, chips):
            last(r, zz).wait_recv()
        focus(n - 1, [r])
        e = (n - 1) * most + r
        copy_y(e, 1).start()
        if r == most - 1:
            copy_x(e, inbox, xnext, 1).start()
        elif relay:

            @pl.when(parity == 1)
            def _():
                copy_x(e, inbox, xdst, 1).start()
        else:
            copy_x(e, inbox, xdst, 1).start()
    pace(n - 2, n - 1 - lag)
    for r in range(most - 1):
        stage_b(n - 1, r)

    def closing(i, _):
        k = n - lag + i // most
        r = lax.rem(i, most)
        r = jnp.where(k == n - 1, most - 1 - r, r)

        @pl.when((k == n - 1) & (r == most - 1))
        def _():
            copy_y(k * most + r, 1).wait_recv()

        stage_c(k, r)
        return 0

    lax.fori_loop(0, lag * most, closing, 0)

    def sent(e, count):
        copy_y(e, count).wait_send()
        copy_x(e, inbox, xdst, count).wait_send()

    def drain(k, _):
        each(k, range(most), sent)
        return 0

    for swap in swaps:
        swap.wait_send()
    for zz in range(1, chips):
        for cc in range(2):
            direct(zz, cc).wait_send()
        for r in range(most):
            last(r, zz).wait_send()

    def drain_step(k, _):
        for zz in range(1, chips):
            step(k, zz).wait_send()
        return 0

    lax.fori_loop(1, n - 1, drain_step, 0)
    for i in range(len(near)):
        near_filter(i).wait_send()
    for i in range(len(far)):
        far_filter(i).wait_send()
    if far:
        for x in (1, 2):
            pass_on(x).wait_send()
            pass_far(x, flipped(day, 3 - x, dates)).wait_send()
    lax.fori_loop(0, n, drain, 0)
    list_copy.wait()


def place(capacity, entry_ref, fil, out_ref, sems):
    def copy(q):
        return pltpu.make_async_copy(fil.at[entry_ref[q]], out_ref.at[q], sems.at[q])

    for q in range(capacity):
        copy(q).start(priority=q % 2)
    for q in range(capacity):
        copy(q).wait()


def body(dates, echo_spectra, range_reference, azimuth_reference, block_owner, block_slot, kernel_index):
    n = lax.axis_size("shard")
    per = block_owner.shape[1] // n
    most = max(2, 2 * per // n)
    capacity = min(2 * per, n * most)
    echo = echo_spectra[0]
    pulses, rng = echo.shape[1:]
    inner = rng // BLK
    mine = rng // BLK // n
    wide = pulses * n
    chips = n // 2
    relay = dates == 4
    parts = dates if relay else 1
    part = wide // parts
    near = (chips // 2 if relay else chips) - 1
    far = chips - 1 - near
    tables = [
        first_table(rng),
        twiddle_table(rng),
        left_table(inner, 1),
        left_table(wide, -1),
        left_table(wide, 1),
        kernel_table(),
        left_table(BLK, -1),
        right_table(BLK, -1),
        left_table(BLK, 1),
        right_table(BLK, 1),
    ]
    smem = pl.BlockSpec(memory_space=pltpu.SMEM)
    hbm = pl.BlockSpec(memory_space=pl.ANY)
    vmem = pl.BlockSpec(memory_space=pltpu.VMEM)
    total = n * most
    box = pltpu.VMEM((total, BLK, 2 * BLK), BF)
    grant = min(60 * 1024 * 1024, 63 * 2**20 - (total + 2) * 4 * BLK * BLK * 2)
    dma = pltpu.SemaphoreType.DMA
    tables = [jnp.asarray(t) for t in tables]
    operands = [block_owner, block_slot, kernel_index, echo, range_reference, azimuth_reference]
    operands += tables
    held = [echo, range_reference] + tables
    filtered, entry = pl.pallas_call(
        functools.partial(kernel, n, dates, most, capacity),
        out_shape=(
            pltpu.VMEM((total + 1, 2, 2, BLK, BLK), BF),
            jax.ShapeDtypeStruct((capacity,), jnp.int32),
        ),
        in_specs=[smem] * 3 + [hbm] * 13,
        out_specs=(vmem, hbm),
        scratch_shapes=[pltpu.SMEM((capacity,), jnp.int32), dma((1,))]
        + [pltpu.VMEM(a.shape, a.dtype) for a in held]
        + [
            pltpu.VMEM((mine, 2, wide, BLK), BF),
            pltpu.SMEM((n * total,), jnp.int32),
            pltpu.SMEM((total,), jnp.int32),
            pltpu.SMEM((total,), jnp.int32),
            pltpu.VMEM((pulses * inner, 2 * BLK), BF),
            pltpu.VMEM((2, pulses, rng // BLK, BLK), F32),
            pltpu.VMEM((2, rng // BLK, pulses, BLK), BF),
            pltpu.VMEM((2, chips - 1, n, most, 2, pulses, BLK), BF),
            pltpu.VMEM((chips, n, most, 2, pulses, BLK), BF),
            pltpu.VMEM((n, n, most, 2, pulses, BLK), BF),
            pltpu.VMEM((n, parts, most, 2, part, BLK), BF),
            pltpu.VMEM((2, near, parts, most, 2, part, BLK), BF),
            pltpu.VMEM((2, max(far, 1), most, 2, part, BLK), BF),
            pltpu.VMEM((parts, most, 2, part, BLK), BF),
            pltpu.VMEM((near, parts, most, 2, part, BLK), BF),
            pltpu.VMEM((max(far, 1), most, 2, part, BLK), BF),
            pltpu.VMEM((most, wide // BLK, BLK, 2 * BLK), BF),
            box,
            box,
            box,
            dma((len(held),)),
            dma((mine,)),
            *[dma((5,))] * 2,
            *[dma((2 * (chips - 1),))] * 2,
            *[dma((n - 1 + most, chips - 1))] * 2,
            *[dma((chips - 1,))] * 2,
            *[dma((4,))] * 2,
            *[dma((total,))] * 4,
        ],
        compiler_params=pltpu.CompilerParams(
            collective_id=0, has_side_effects=True, vmem_limit_bytes=grant
        ),
    )(
        *operands
    )
    out = pl.pallas_call(
        functools.partial(place, capacity),
        out_shape=jax.ShapeDtypeStruct((capacity, 2, 2, BLK, BLK), BF),
        in_specs=[smem, vmem],
        out_specs=hbm,
        scratch_shapes=[dma((capacity,))],
        compiler_params=pltpu.CompilerParams(vmem_limit_bytes=grant),
    )(entry, pltpu.with_memory_space_constraint(filtered, pltpu.VMEM))
    return out[None]


def solution(mesh):
    in_specs = (
        P(("grp", "date"), None, "shard", None),
        P(),
        P(None, None, "shard"),
        P(("grp", "date"), None),
        P(("grp", "date"), None),
        P(("grp", "date"), None),
    )
    out_specs = P(("grp", "date"), "shard", None, None, None, None)
    return jax.shard_map(
        functools.partial(body, mesh.shape["date"]),
        mesh=mesh,
        in_specs=in_specs,
        out_specs=out_specs,
        check_vma=False,
    )
```

```python
import functools
import math

import jax
import jax.numpy as jnp
import ml_dtypes
import numpy as np
from jax import lax
from jax.experimental import pallas as pl
from jax.experimental.pallas import tpu as pltpu
from jax.sharding import PartitionSpec as P

BLK = 128
NSUB = 8
WORD = 4
BF = jnp.bfloat16
F32 = jnp.float32


def dft_parts(size, sign):
    index = np.arange(size)
    angle = 2.0 * math.pi / size * (index[:, None] * index[None, :] % size)
    scale = 1.0 / math.sqrt(size)
    return np.cos(angle) * scale, sign * np.sin(angle) * scale


def left_table(size, sign):
    cosine, sine = dft_parts(size, sign)
    return np.block([[cosine, -sine], [sine, cosine]]).astype(ml_dtypes.bfloat16)


def right_table(size, sign):
    return np.ascontiguousarray(left_table(size, sign).T)


def first_table(rng):
    outer, inner = BLK, rng // BLK
    low = outer * BLK // rng
    cosine, sine = dft_parts(outer, 1)
    full = np.stack([np.stack([cosine, sine], 1), np.stack([-sine, cosine], 1)])
    full = full.reshape(2, outer // low, low, 2 * outer)
    return np.transpose(full, (2, 0, 1, 3)).reshape(2 * outer, 2 * outer).astype(ml_dtypes.bfloat16)


def twiddle_table(rng):
    inner = rng // BLK
    phase = np.arange(inner)[:, None] * np.arange(BLK)[None, :] % rng
    angle = 2.0 * math.pi / rng * phase
    return np.stack([np.cos(angle), np.sin(angle)]).astype(np.float32)


def kernel_table():
    offset = (np.arange(NSUB) + 0.5) / NSUB
    cells = np.arange(BLK)
    dist = cells[None, None, :] - cells[None, :, None] - offset[:, None, None]
    window = np.where(np.abs(dist) < 4.0, 0.5 + 0.5 * np.cos(math.pi * dist / 4.0), 0.0)
    return (np.sinc(dist) * window).astype(ml_dtypes.bfloat16)


def flipped(a, b, n):
    total = 0
    bit = 1
    while bit < n:
        total = total + (a // bit + b // bit) % 2 * bit
        bit *= 2
    return total


def mm(left, right):
    return jnp.dot(left, right, preferred_element_type=F32)


def kernel(
    n,
    dates,
    most,
    capacity,
    owner_ref,
    slot_ref,
    kinds_ref,
    echo_hbm,
    rref_hbm,
    aref_hbm,
    t1_hbm,
    tw_hbm,
    w2_hbm,
    pf_hbm,
    pb_hbm,
    kt_hbm,
    gfl_hbm,
    gfr_hbm,
    gbl_hbm,
    gbr_hbm,
    fil,
    entry_out,
    entry_ref,
    sl,
    echo_ref,
    rref_ref,
    t1_ref,
    tw_ref,
    w2_ref,
    pf_ref,
    pb_ref,
    kt_ref,
    gfl_ref,
    gfr_ref,
    gbl_ref,
    gbr_ref,
    ats,
    tile_ref,
    kind_ref,
    row_ref,
    lhs,
    mat,
    snd,
    mix,
    xch,
    xin,
    azin,
    azm,
    azf,
    azx0,
    azx1,
    azx2,
    img,
    inbox,
    ybox,
    xbox,
    si,
    sa,
    se,
    re,
    sd,
    rd,
    sz,
    rz,
    saz,
    raz,
    sf,
    rf,
    sy,
    ry,
    sx,
    rx,
):
    me = lax.axis_index("shard")
    day = lax.axis_index("date")
    grp = lax.axis_index("grp")
    relay = dates == 4
    parity = lax.rem(day, 2)
    ydst = lax.rem(day + dates - 2, dates)
    xnext = lax.rem(day + dates - 1, dates)
    xdst = day + 1 - 2 * parity if relay else xnext
    mesh_id = pl.DeviceIdType.MESH

    barrier = pltpu.get_barrier_semaphore()

    def greet(k, _):
        pl.semaphore_signal(
            barrier, inc=1, device_id=(grp, day, flipped(me, n - k, n)), device_id_type=mesh_id
        )
        return 0

    lax.fori_loop(1, n, greet, 0)
    if relay:
        others = [flipped(day, x, dates) for x in range(1, dates)]
    else:
        others = [lax.rem(day + 2, dates), lax.rem(day + 1, dates)]
    for other in others:
        pl.semaphore_signal(barrier, inc=1, device_id=(grp, other, me), device_id_type=mesh_id)

    pulses = echo_ref.shape[1]
    rng = echo_ref.shape[2]
    tiles = rng // BLK
    inner = rng // BLK
    mine = tiles // n
    wide = n * pulses
    rows_of = wide // BLK
    chips = n // 2
    total = n * most
    per = owner_ref.shape[1] // n
    parts = azin.shape[1]
    part = wide // parts
    near = list(range(1, chips // 2 if relay else chips))
    far = list(range(chips // 2, chips)) if relay else []

    loads = [
        pltpu.make_async_copy(a, b, si.at[i])
        for i, (a, b) in enumerate(
            [
                (echo_hbm, echo_ref),
                (rref_hbm, rref_ref),
                (t1_hbm, t1_ref),
                (tw_hbm, tw_ref),
                (w2_hbm, w2_ref),
                (pf_hbm, pf_ref),
                (pb_hbm, pb_ref),
                (kt_hbm, kt_ref),
                (gfl_hbm, gfl_ref),
                (gfr_hbm, gfr_ref),
                (gbl_hbm, gbl_ref),
                (gbr_hbm, gbr_ref),
            ]
        )
    ]
    slabs = [
        pltpu.make_async_copy(aref_hbm.at[:, :, pl.ds(t * BLK, BLK)], ats.at[t], sa.at[t])
        for t in range(mine)
    ]
    for load in loads[:5] + slabs + loads[5:]:
        load.start()

    bits = 32 // WORD
    words = (n + bits - 1) // bits

    def sources(g, _):
        packed = [[jnp.int32(0)] * most for _ in range(words)]
        for b in range(per):
            owner = owner_ref[0, g * per + b]
            for w in range(words):
                shift = (owner - w * bits) * WORD
                live = None
                if words > 1:
                    live = owner // bits == w
                    shift = jnp.where(live, shift, 0)
                for r in range(most):
                    empty = ((packed[w][r] >> shift) & (2**WORD - 1)) == 0
                    put = empty if live is None else live & empty
                    packed[w][r] = packed[w][r] | jnp.where(put, (b + 1) << shift, 0)
                    live = ~empty if live is None else live & ~empty
        for w in range(words):
            for x in range(w * bits, min(n, (w + 1) * bits)):
                flip = flipped(me, x, n)
                for r in range(most):
                    found = (packed[w][r] >> ((x - w * bits) * WORD)) & (2**WORD - 1)
                    found = jnp.maximum(found - 1, 0)
                    tile_ref[(flip * n + flipped(g, x, n)) * most + r] = g * mine + lax.rem(found, mine)
        return 0

    lax.fori_loop(0, n, sources, 0)

    def entries(t, held):
        held = list(held)
        at = flipped(me, t, n) * most
        found = [jnp.int32(0)] * most
        seen = jnp.int32(0)
        for b in range(per):
            named = owner_ref[0, t * per + b] == me
            for r in range(most):
                found[r] = jnp.where(named & (seen == r), b, found[r])
            seen = seen + named.astype(jnp.int32)
        for r in range(most):
            row_ref[at + r] = found[r] // mine
            kind_ref[at + r] = kinds_ref[0, t * per + found[r]]
        for b in range(per):
            named = owner_ref[0, t * per + b] == me
            slot = jnp.where(named, slot_ref[0, t * per + b], -1)
            for q in range(capacity):
                held[q] = jnp.where(slot == q, at, held[q])
            at = at + named.astype(jnp.int32)
        return tuple(held)

    for load in loads[:5]:
        load.wait()
    real = echo_ref[0].astype(F32)
    imag = echo_ref[1].astype(F32)
    rre = rref_ref[0:1, :]
    rim = rref_ref[1:2, :]
    mat[0] = (real * rre + imag * rim).reshape(pulses, tiles, BLK)
    mat[1] = (imag * rre - real * rim).reshape(pulses, tiles, BLK)

    for p in range(pulses):
        both = jnp.concatenate([mat[0, p], mat[1, p]], axis=0).T
        low = BLK // inner
        pieces = [both[x * inner : (x + 1) * inner] for x in range(low)]
        lhs[p * inner : (p + 1) * inner, :] = jnp.concatenate(pieces, axis=1).astype(BF)

    twc = tw_ref[0]
    tws = tw_ref[1]
    group = 4
    for g in range(0, pulses, group):
        section = mm(lhs[g * inner : (g + group) * inner, :], t1_ref[...])
        rights = []
        for p in range(group):
            sre = section[p * inner : (p + 1) * inner, :BLK]
            sim = section[p * inner : (p + 1) * inner, BLK:]
            rights.append(
                jnp.concatenate([sre * twc - sim * tws, sre * tws + sim * twc], axis=0).astype(BF)
            )
        second = mm(w2_ref[...], jnp.concatenate(rights, axis=1))
        for p in range(group):
            mat[:, g + p] = second[:, p * BLK : (p + 1) * BLK].reshape(2, tiles, BLK)
    for c in range(2):
        snd[c] = jnp.swapaxes(mat[c], 0, 1).astype(BF)

    def gather(k, _):
        for zz in range(chips):
            for cc in range(2):
                for r in range(most):
                    piece = snd[:, tile_ref[((2 * zz + cc) * n + k) * most + r]]
                    if cc:
                        xch[zz, k, r] = piece
                    elif zz:
                        mix[0, zz - 1, k, r] = piece
                    else:
                        xin[0, k, r] = piece
        return 0

    gather(0, 0)

    for slab in slabs:
        slab.wait()

    def filters(j, r):
        return ats.at[tile_ref[(j * n + j) * most + r] - me * mine]

    for r in range(most):
        for i, zz in enumerate(far):
            rows = pl.ds(pl.multiple_of(day * part, part), part)
            azf[0, i, r] = filters(2 * zz, r)[:, rows]
            azx2[i, r] = filters(2 * zz + 1, r)[:, rows]

    pl.semaphore_wait(barrier, n - 1 + len(others))

    def remote(src, dst, send, recv, to_day, flip):
        return pltpu.make_async_remote_copy(
            src_ref=src,
            dst_ref=dst,
            send_sem=send,
            recv_sem=recv,
            device_id=(grp, to_day, me if flip is None else flipped(me, flip, n)),
            device_id_type=mesh_id,
        )

    swaps = [
        remote(xch.at[pl.ds(1, chips - 1)], mix.at[1], se.at[0], re.at[0], day, 1),
        remote(xch.at[0], xin.at[1], se.at[1], re.at[1], day, 1),
        remote(azx0, azin.at[1], se.at[2], re.at[2], day, 1),
        remote(azx1, azm.at[1], se.at[3], re.at[3], day, 1),
    ]
    if far:
        swaps.append(remote(azx2, azf.at[1], se.at[4], re.at[4], day, 1))

    def direct(zz, cc):
        i = 2 * (zz - 1) + cc
        src = xch.at[zz, 0] if cc else mix.at[0, zz - 1, 0]
        return remote(src, xin.at[2 * zz + cc, 0], sd.at[i], rd.at[i], day, 2 * zz + cc)

    def step(k, zz, count=1):
        span = pl.ds(k, count)
        return remote(
            mix.at[:, zz - 1, span],
            xin.at[pl.ds(2 * zz, 2), span],
            sz.at[k, zz - 1],
            rz.at[k, zz - 1],
            day,
            2 * zz,
        )

    def last(r, zz):
        return remote(
            mix.at[:, zz - 1, n - 1, r],
            xin.at[pl.ds(2 * zz, 2), n - 1, r],
            sz.at[n - 1 + r, zz - 1],
            rz.at[n - 1 + r, zz - 1],
            day,
            2 * zz,
        )

    def near_filter(i):
        zz = near[i]
        return remote(
            azm.at[:, i], azin.at[pl.ds(2 * zz, 2)], saz.at[zz - 1], raz.at[zz - 1], day, 2 * zz
        )

    def far_filter(i):
        zz = far[i]
        return remote(
            azf.at[:, i],
            azin.at[pl.ds(2 * zz, 2), day],
            saz.at[zz - 1],
            raz.at[zz - 1],
            day,
            2 * zz,
        )

    def pass_on(x):
        slab = azin.at[pl.ds(n // 2, n // 2), day]
        return remote(slab, slab, sf.at[x - 1], rf.at[x - 1], flipped(day, x, dates), None)

    def pass_far(x, held):
        half = azin.at[pl.ds(n // 2 + (2 - x) * (n // 4), n // 4), held]
        return remote(half, half, sf.at[x + 1], rf.at[x + 1], flipped(day, x, dates), None)

    for zz in range(chips - 1, 0, -1):
        for cc in range(2):
            direct(zz, cc).start()
    for swap in swaps[4:]:
        swap.start()
    lax.fori_loop(1, n, gather, 0)
    swaps[1].start()
    swaps[0].start()
    for r in range(most):
        for d in range(parts):
            rows = slice(d * part, (d + 1) * part)
            azin[0, d, r] = filters(0, r)[:, rows]
            azx0[d, r] = filters(1, r)[:, rows]
            for i, zz in enumerate(near):
                azm[0, i, d, r] = filters(2 * zz, r)[:, rows]
                azx1[i, d, r] = filters(2 * zz + 1, r)[:, rows]
    for swap in swaps[2:4]:
        swap.start()
    for swap in swaps[4:]:
        swap.wait_recv()
    for i in range(len(far)):
        far_filter(i).start()
    swaps[0].wait_recv()
    for zz in range(chips - 1, 0, -1):
        step(1, zz).start()
    swaps[3].wait_recv()
    for i in range(len(near)):
        near_filter(i).start()

    def start_step(k, _):
        for zz in range(chips - 1, 0, -1):
            step(k, zz).start()
        return 0

    lax.fori_loop(2, n - 1, start_step, 0)
    for r in range(most):
        for zz in range(chips - 1, 0, -1):
            last(r, zz).start()

    held = lax.fori_loop(0, n, entries, (jnp.int32(total),) * capacity)
    for q in range(capacity):
        entry_ref[q] = held[q]
    list_copy = pltpu.make_async_copy(entry_ref, entry_out, sl.at[0])
    list_copy.start()
    fil[total] = jnp.zeros_like(fil[total])

    for load in loads[5:]:
        load.wait()

    joined = 0

    def copy_y(e, count):
        span = pl.ds(e, count)
        return remote(inbox.at[span], ybox.at[span], sy.at[e], ry.at[e], ydst, None)

    def copy_x(e, source, to, count):
        span = pl.ds(e, count)
        return remote(source.at[span], xbox.at[span], sx.at[e], rx.at[e], to, None)

    def focus(k, picks):
        columns = []
        filt = []
        for r in picks:
            pieces = [
                xin[flipped(me, s, n), k, r, c] for c in range(2) for s in range(n)
            ]
            columns.append(jnp.concatenate(pieces, axis=0))
            filt.append(
                [
                    jnp.concatenate([azin[k, d, r, c] for d in range(parts)], axis=0)
                    for c in range(2)
                ]
            )
        doppler = mm(pf_ref[...], jnp.concatenate(columns, axis=1))
        are = jnp.concatenate([f[0] for f in filt], axis=1).astype(F32)
        aim = jnp.concatenate([f[1] for f in filt], axis=1).astype(F32)
        dre = doppler[:wide]
        dim = doppler[wide:]
        shaped = jnp.concatenate([dre * are - dim * aim, dre * aim + dim * are], axis=0).astype(BF)
        image = mm(pb_ref[...], shaped).astype(BF)
        for i, r in enumerate(picks):
            e = k * most + r
            block = [
                jnp.concatenate(
                    [
                        image[c * wide + y * BLK : c * wide + (y + 1) * BLK, i * BLK : (i + 1) * BLK]
                        for c in range(2)
                    ],
                    axis=1,
                )
                for y in range(rows_of)
            ]
            if rows_of > 1:
                for y in range(rows_of):
                    img[i, y] = block[y]
                block = [img[i, row_ref[e]]]
            inbox[e] = mm(kt_ref[kind_ref[e]], block[0]).astype(BF)

    def stage_a(k):
        @pl.when(k == 0)
        def _():
            swaps[1].wait_recv()
            for zz in range(1, chips):
                for cc in range(2):
                    direct(zz, cc).wait_recv()

        @pl.when(k > 0)
        def _():
            for zz in range(1, chips):
                step(k, zz).wait_recv()

        @pl.when(k == 1)
        def _():
            swaps[2].wait_recv()

        for i, zz in enumerate(near):

            @pl.when(k == 2 * zz)
            def _():
                near_filter(i).wait_recv()

        if far:

            @pl.when(k == n // 2)
            def _():
                for x in (1, 2):
                    pass_far(x, flipped(day, 3, dates)).wait_recv()

        focus(k, range(most))

        def send(e, count):
            copy_y(e, count).start()
            if relay:

                @pl.when(parity == 1)
                def _():
                    copy_x(e, inbox, xdst, count).start()
            else:
                copy_x(e, inbox, xdst, count).start()

        each(k, range(most), send)

    def each(k, picks, act):
        for r in picks:

            @pl.when((k < joined) & (r == 0))
            def _():
                act(k * most, most)

            @pl.when(k >= joined)
            def _():
                act(k * most + r, 1)

    def stage_b(k, r):
        def onward(e, count):
            copy_y(e, count).wait_recv()
            if relay:

                @pl.when(parity == 0)
                def _():
                    copy_x(e, ybox, xdst, count).start()

        each(k, [r], onward)

    def patches(at):
        own = inbox[at].astype(F32)
        ore = own[:, :BLK]
        oim = own[:, BLK:]
        tops = []
        lows = []
        for box in (xbox, ybox):
            oth = box[at].astype(F32)
            tre = oth[:, :BLK]
            tim = oth[:, BLK:]
            tops.append(ore * tre + oim * tim)
            lows.append(oim * tre - ore * tim)
        pair = jnp.concatenate(
            [jnp.concatenate(tops, axis=1), jnp.concatenate(lows, axis=1)], axis=0
        ).astype(BF)

        def turned(x):
            return jnp.concatenate(
                [
                    jnp.concatenate([x[:BLK, :BLK], x[BLK:, :BLK]], axis=1),
                    jnp.concatenate([x[:BLK, BLK:], x[BLK:, BLK:]], axis=1),
                ],
                axis=0,
            )

        rows = mm(gfl_ref[...], pair).astype(BF)
        spectrum = mm(turned(rows), gfr_ref[...])
        weighted = []
        for x in range(2):
            spec = spectrum[x * BLK : (x + 1) * BLK]
            sre = spec[:, :BLK]
            sim = spec[:, BLK:]
            power = sre * sre + sim * sim
            line = power + pltpu.roll(power, 1, 1) + pltpu.roll(power, BLK - 1, 1)
            smooth = line + pltpu.roll(line, 1, 0) + pltpu.roll(line, BLK - 1, 0)
            level = jnp.sum(jnp.sum(power, axis=0, keepdims=True), axis=1, keepdims=True)
            level = 9.0 * (level * (1.0 / (BLK * BLK)) + 1e-06)
            weight = lax.rsqrt(lax.rsqrt(smooth * (1.0 / level)))
            weighted.append(jnp.concatenate([sre * weight, sim * weight], axis=1))
        weighted = jnp.concatenate(weighted, axis=0).astype(BF)
        back = mm(gbl_ref[...], turned(weighted)).astype(BF)
        done = mm(turned(back), gbr_ref[...]).astype(BF)
        for x in range(2):
            for c in range(2):
                fil[at, x, c] = done[x * BLK : (x + 1) * BLK, c * BLK : (c + 1) * BLK]

    def stage_c(k, r):
        each(k, [r], lambda e, count: copy_x(e, inbox, xdst, count).wait_recv())
        patches(k * most + r)

    def pace(kb, kc):
        def one(r, _):
            @pl.when(kc >= 0)
            def _():
                stage_c(kc, r)

            @pl.when(kb >= 0)
            def _():
                stage_b(kb, r)

            return 0

        lax.fori_loop(0, most, one, 0)

    lag = 2

    def main(t, _):
        stage_a(t)
        pace(t - 1, t - lag)
        if far:

            @pl.when(t == 0)
            def _():
                for i in range(len(far)):
                    far_filter(i).wait_recv()
                for x in (1, 2):
                    pass_on(x).start()

            @pl.when(t == 1)
            def _():
                for x in (1, 2):
                    pass_on(3 - x).wait_recv()
                    pass_far(x, flipped(day, 3 - x, dates)).start()

        return 0

    lax.fori_loop(0, n - 1, main, 0)
    for r in range(most):
        for zz in range(1, chips):
            last(r, zz).wait_recv()
        focus(n - 1, [r])
        e = (n - 1) * most + r
        copy_y(e, 1).start()
        if r == most - 1:
            copy_x(e, inbox, xnext, 1).start()
        elif relay:

            @pl.when(parity == 1)
            def _():
                copy_x(e, inbox, xdst, 1).start()
        else:
            copy_x(e, inbox, xdst, 1).start()
    pace(n - 2, n - 1 - lag)
    for r in range(most - 1):
        stage_b(n - 1, r)

    def closing(i, _):
        k = n - lag + i // most
        r = lax.rem(i, most)
        r = jnp.where(k == n - 1, most - 1 - r, r)

        @pl.when((k == n - 1) & (r == most - 1))
        def _():
            copy_y(k * most + r, 1).wait_recv()

        stage_c(k, r)
        return 0

    lax.fori_loop(0, lag * most, closing, 0)

    def sent(e, count):
        copy_y(e, count).wait_send()
        copy_x(e, inbox, xdst, count).wait_send()

    def drain(k, _):
        each(k, range(most), sent)
        return 0

    for swap in swaps:
        swap.wait_send()
    for zz in range(1, chips):
        for cc in range(2):
            direct(zz, cc).wait_send()
        for r in range(most):
            last(r, zz).wait_send()

    def drain_step(k, _):
        for zz in range(1, chips):
            step(k, zz).wait_send()
        return 0

    lax.fori_loop(1, n - 1, drain_step, 0)
    for i in range(len(near)):
        near_filter(i).wait_send()
    for i in range(len(far)):
        far_filter(i).wait_send()
    if far:
        for x in (1, 2):
            pass_on(x).wait_send()
            pass_far(x, flipped(day, 3 - x, dates)).wait_send()
    lax.fori_loop(0, n, drain, 0)
    list_copy.wait()


def place(capacity, entry_ref, fil, out_ref, sems):
    def copy(q):
        return pltpu.make_async_copy(fil.at[entry_ref[q]], out_ref.at[q], sems.at[q])

    for q in range(capacity):
        copy(q).start(priority=q % 2)
    for q in range(capacity):
        copy(q).wait()


def body(dates, echo_spectra, range_reference, azimuth_reference, block_owner, block_slot, kernel_index):
    n = lax.axis_size("shard")
    per = block_owner.shape[1] // n
    most = max(2, 2 * per // n)
    capacity = min(2 * per, n * most)
    echo = echo_spectra[0]
    pulses, rng = echo.shape[1:]
    inner = rng // BLK
    mine = rng // BLK // n
    wide = pulses * n
    chips = n // 2
    relay = dates == 4
    parts = dates if relay else 1
    part = wide // parts
    near = (chips // 2 if relay else chips) - 1
    far = chips - 1 - near
    tables = [
        first_table(rng),
        twiddle_table(rng),
        left_table(inner, 1),
        left_table(wide, -1),
        left_table(wide, 1),
        kernel_table(),
        left_table(BLK, -1),
        right_table(BLK, -1),
        left_table(BLK, 1),
        right_table(BLK, 1),
    ]
    smem = pl.BlockSpec(memory_space=pltpu.SMEM)
    hbm = pl.BlockSpec(memory_space=pl.ANY)
    vmem = pl.BlockSpec(memory_space=pltpu.VMEM)
    total = n * most
    box = pltpu.VMEM((total, BLK, 2 * BLK), BF)
    grant = min(60 * 1024 * 1024, 63 * 2**20 - (total + 2) * 4 * BLK * BLK * 2)
    dma = pltpu.SemaphoreType.DMA
    tables = [jnp.asarray(t) for t in tables]
    operands = [block_owner, block_slot, kernel_index, echo, range_reference, azimuth_reference]
    operands += tables
    held = [echo, range_reference] + tables
    filtered, entry = pl.pallas_call(
        functools.partial(kernel, n, dates, most, capacity),
        out_shape=(
            pltpu.VMEM((total + 1, 2, 2, BLK, BLK), BF),
            jax.ShapeDtypeStruct((capacity,), jnp.int32),
        ),
        in_specs=[smem] * 3 + [hbm] * 13,
        out_specs=(vmem, hbm),
        scratch_shapes=[pltpu.SMEM((capacity,), jnp.int32), dma((1,))]
        + [pltpu.VMEM(a.shape, a.dtype) for a in held]
        + [
            pltpu.VMEM((mine, 2, wide, BLK), BF),
            pltpu.SMEM((n * total,), jnp.int32),
            pltpu.SMEM((total,), jnp.int32),
            pltpu.SMEM((total,), jnp.int32),
            pltpu.VMEM((pulses * inner, 2 * BLK), BF),
            pltpu.VMEM((2, pulses, rng // BLK, BLK), F32),
            pltpu.VMEM((2, rng // BLK, pulses, BLK), BF),
            pltpu.VMEM((2, chips - 1, n, most, 2, pulses, BLK), BF),
            pltpu.VMEM((chips, n, most, 2, pulses, BLK), BF),
            pltpu.VMEM((n, n, most, 2, pulses, BLK), BF),
            pltpu.VMEM((n, parts, most, 2, part, BLK), BF),
            pltpu.VMEM((2, near, parts, most, 2, part, BLK), BF),
            pltpu.VMEM((2, max(far, 1), most, 2, part, BLK), BF),
            pltpu.VMEM((parts, most, 2, part, BLK), BF),
            pltpu.VMEM((near, parts, most, 2, part, BLK), BF),
            pltpu.VMEM((max(far, 1), most, 2, part, BLK), BF),
            pltpu.VMEM((most, wide // BLK, BLK, 2 * BLK), BF),
            box,
            box,
            box,
            dma((len(held),)),
            dma((mine,)),
            *[dma((5,))] * 2,
            *[dma((2 * (chips - 1),))] * 2,
            *[dma((n - 1 + most, chips - 1))] * 2,
            *[dma((chips - 1,))] * 2,
            *[dma((4,))] * 2,
            *[dma((total,))] * 4,
        ],
        compiler_params=pltpu.CompilerParams(
            collective_id=0, has_side_effects=True, vmem_limit_bytes=grant
        ),
    )(
        *operands
    )
    out = pl.pallas_call(
        functools.partial(place, capacity),
        out_shape=jax.ShapeDtypeStruct((capacity, 2, 2, BLK, BLK), BF),
        in_specs=[smem, vmem],
        out_specs=hbm,
        scratch_shapes=[dma((capacity,))],
        compiler_params=pltpu.CompilerParams(vmem_limit_bytes=grant),
    )(entry, pltpu.with_memory_space_constraint(filtered, pltpu.VMEM))
    return out[None]


def solution(mesh):
    in_specs = (
        P(("grp", "date"), None, "shard", None),
        P(),
        P(None, None, "shard"),
        P(("grp", "date"), None),
        P(("grp", "date"), None),
        P(("grp", "date"), None),
    )
    out_specs = P(("grp", "date"), "shard", None, None, None, None)
    return jax.shard_map(
        functools.partial(body, mesh.shape["date"]),
        mesh=mesh,
        in_specs=in_specs,
        out_specs=out_specs,
        check_vma=False,
    )
```
